128 devices in a mesh: member: 4 (over y_lo, core), band: 32 (over y_hi, x, z).
Axes of the slice: x: 4, y: 4 (y_hi: 2, y_lo: 2; y = y_hi * 2 + y_lo), z: 4, core: 2. Of those that a mesh axis runs over, the one named last changes fastest.
Arguments:
- starting_condition: bfloat16 [16, 256, 64, 1440], P('member', 'band'), may hold values from -6 to 6
- filter_kernel_tensor: bfloat16 [3, 3, 64, 64], replicated, may hold values from -0.25 to 0.25
- filter_offset_vector: float32 [64], replicated, may hold values from -3 to 3
- measured_cell_position: int32 [65536], P('band'), may hold values from 0 to 737279
- measured_slot_number: int32 [32], P('band'), may hold values from 512 to 2048, as said below
- measured_reading: float32 [65536], P('band'), may hold values from -6 to 6
- measured_precision_factor: float32 [65536], P('band'), may hold values from 0.002 to 0.02
Outputs:
- analysis: bfloat16 [16, 256, 64, 1440], P('member', 'band')
The draws below stay inside these ranges and needn't reach their ends.
Inputs may be any that keep to these rules, and one draw needn't show every extreme that they name: `measured_slot_number`: some band has all 2048 slots live.
All inputs are finite; a program needn't handle non-finite values.
Results may differ from the reference program's by a relative error of at most 0.0071.
Values may be sent and summed in bfloat16 or wider, within the bound.
A program may use at most 192 MiB of HBM per device.

```python
import math
import jax
import jax.numpy as jnp
from jax import lax

PHYSICAL_VARS = 64
GRID_MERIDIANS = 1440
STRIP_PARALLELS = 8
OBS_DEV = 2048
STEPS = 2
NS_STEPS = 16
ENSEMBLE_SIZE = 16
GRID_PARALLELS = 256
OBS_ALL = 65536


def draw_measured_slot_number(key, part):
    meridional_strips = GRID_PARALLELS // STRIP_PARALLELS
    first_key, second_key = jax.random.split(jax.random.fold_in(key, 7))
    counts = jax.random.randint(first_key, (meridional_strips,), OBS_DEV // 4, OBS_DEV + 1)
    filled = jax.random.randint(second_key, (), 0, meridional_strips)
    return jnp.where(jnp.arange(meridional_strips) == filled, OBS_DEV, counts).astype(jnp.int32)


def draw_starting_condition(key, part):
    base_key = jax.random.fold_in(key, 11)
    coefficient_key, common_key, field_key = jax.random.split(base_key, 3)
    field_shape = (GRID_PARALLELS, PHYSICAL_VARS, GRID_MERIDIANS)
    mixture = 0.5 * jnp.eye(ENSEMBLE_SIZE, dtype=jnp.float32) + 0.25 * jax.random.normal(coefficient_key, (ENSEMBLE_SIZE, ENSEMBLE_SIZE), jnp.float32)
    common_field = 0.5 * jax.random.normal(common_key, field_shape, jnp.float32)
    accumulated = jnp.broadcast_to(common_field[None], (ENSEMBLE_SIZE,) + field_shape)

    def add_field(position, running):
        source_field = jax.random.normal(jax.random.fold_in(field_key, position), field_shape, jnp.float32)
        column = lax.dynamic_slice_in_dim(mixture, position, 1, 1)
        return running + column[:, :, None, None] * source_field[None]
    accumulated = lax.fori_loop(0, ENSEMBLE_SIZE, add_field, accumulated)
    return jnp.clip(accumulated, -6.0, 6.0).astype(jnp.bfloat16)


def touch_ends(values, key, smallest, high):
    shape = values.shape
    index_at = [jax.random.randint(jax.random.fold_in(key, axis), (), 0, shape[axis]) for axis in range(len(shape))]
    values = values.at[tuple(index_at)].set(smallest)
    longest = shape.index(max(shape))
    index_at[longest] = (index_at[longest] + 1) % shape[longest]
    return values.at[tuple(index_at)].set(high)


def level_of(own_key, shape, shards, smallest, largest):
    def one(axis_at, parts):
        steps = jax.random.uniform(jax.random.fold_in(jax.random.fold_in(own_key, 6), axis_at), (parts,), jnp.float32, smallest / len(shards), largest / len(shards))
        return jnp.repeat(jnp.exp(steps), shape[axis_at] // parts).reshape((-1,) + (1,) * (len(shape) - axis_at - 1))

    level = one(*shards[0])
    for cut in shards[1:]:
        level = level * one(*cut)
    return level


def scatter_about(stream_key, shape, deviation, reach, shards=(), kind=jnp.bfloat16):
    result = deviation * jax.random.normal(stream_key, shape, jnp.float32)
    if shards:
        result = result * level_of(stream_key, shape, shards, -0.22, 0.18)
    return jnp.clip(result, -reach, reach).astype(kind)


def setup_inputs(seed: int = 0) -> dict:
    keys = jax.random.split(jax.random.key(seed), 8)
    starting_condition = draw_starting_condition(jax.random.fold_in(keys[7], 71), 0)
    filter_kernel_tensor = scatter_about(keys[1], (3, 3, PHYSICAL_VARS, PHYSICAL_VARS), (9 * PHYSICAL_VARS) ** -0.5, 0.25)
    filter_offset_vector = scatter_about(keys[2], (PHYSICAL_VARS,), 0.5, 3.0, (), jnp.float32)
    measured_cell_position = touch_ends(jax.random.randint(keys[3], (OBS_ALL,), 0, STRIP_PARALLELS * PHYSICAL_VARS * GRID_MERIDIANS), jax.random.fold_in(keys[3], 1), 0, (STRIP_PARALLELS * PHYSICAL_VARS * GRID_MERIDIANS) - 1).astype(jnp.int32)
    measured_slot_number = draw_measured_slot_number(jax.random.fold_in(keys[7], 71), 0)
    measured_reading = scatter_about(keys[5], (OBS_ALL,), 1.0, 6.0, ((0, 32),), jnp.float32)
    measured_precision_factor = jnp.clip(jnp.exp(math.log(0.02) - 2.30258502 * jax.random.uniform(keys[6], (OBS_ALL,), jnp.float32) ** level_of(keys[6], (OBS_ALL,), ((0, 32),), -0.2, 0.2)), 0.002, 0.02)
    return {"starting_condition": starting_condition, "filter_kernel_tensor": filter_kernel_tensor, "filter_offset_vector": filter_offset_vector, "measured_cell_position": measured_cell_position, "measured_slot_number": measured_slot_number, "measured_reading": measured_reading, "measured_precision_factor": measured_precision_factor}


def kernel_mats(filter_kernel_tensor):
    width = filter_kernel_tensor.shape[2]
    return [jnp.transpose(filter_kernel_tensor[offset], (1, 0, 2)).reshape(width, 3 * width) for offset in range(3)]

def step_fields(model_grids, filter_kernel_tensor, filter_offset_vector):
    matrices = kernel_mats(filter_kernel_tensor)
    padded = jnp.pad(model_grids, ((1, 1), (0, 0), (0, 0)))
    stacked = jnp.concatenate([jnp.roll(padded, 1, axis=2), padded, jnp.roll(padded, -1, axis=2)], axis=1).astype(jnp.float32)
    height = model_grids.shape[0]
    total = jnp.zeros(model_grids.shape, jnp.float32)
    for offset in range(3):
        total = total + jnp.einsum('oc,rcl->rol', matrices[offset].astype(jnp.float32), stacked[offset:offset + height])
    return (model_grids.astype(jnp.float32) + jnp.tanh(total + filter_offset_vector[None, :, None])).astype(jnp.bfloat16)

def transform(gram, drive, ensemble_vectors):
    highest = lax.Precision.HIGHEST
    eye = jnp.eye(ensemble_vectors, dtype=jnp.float32)
    system = eye + gram / (ensemble_vectors - 1.0)
    scale = jnp.trace(system)
    iterate = system / scale
    root = eye
    for number in range(NS_STEPS):
        factor = 0.5 * (3.0 * eye - jnp.dot(root, iterate, precision=highest))
        iterate = jnp.dot(iterate, factor, precision=highest)
        root = jnp.dot(factor, root, precision=highest)
    spread = root / jnp.sqrt(scale)
    inverse = jnp.dot(root, root, precision=highest)
    mean_weights = jnp.dot(inverse, drive, precision=highest) / (scale * (ensemble_vectors - 1.0))
    centering = eye - 1.0 / ensemble_vectors
    mixing = 1.0 / ensemble_vectors + jnp.dot(centering, mean_weights[:, None] + spread, precision=highest)
    return mixing.astype(jnp.bfloat16)

def reference(starting_condition, filter_kernel_tensor, filter_offset_vector, measured_cell_position, measured_slot_number, measured_reading, measured_precision_factor):

    def advance_single_run(model_grids):
        for number in range(STEPS):
            model_grids = step_fields(model_grids, filter_kernel_tensor, filter_offset_vector)
        return model_grids
    predicted_grids = lax.map(advance_single_run, starting_condition)
    ensemble_vectors = predicted_grids.shape[0]
    meridional_strips = GRID_PARALLELS // STRIP_PARALLELS
    unrolled_vector = predicted_grids.reshape(ensemble_vectors, GRID_PARALLELS * PHYSICAL_VARS * GRID_MERIDIANS)
    offsets = (jnp.arange(meridional_strips, dtype=jnp.int32) * (STRIP_PARALLELS * PHYSICAL_VARS * GRID_MERIDIANS))[:, None]
    global_index = (measured_cell_position.reshape(meridional_strips, OBS_DEV) + offsets).reshape(-1).astype(jnp.int32)
    predicted = jnp.take(unrolled_vector, global_index, axis=1).astype(jnp.float32)
    slots = jnp.arange(OBS_DEV, dtype=jnp.int32)
    live = (slots[None, :] < measured_slot_number[:, None]).reshape(-1).astype(jnp.float32)
    mean = lax.optimization_barrier(jnp.mean(predicted, axis=0))
    anomaly = predicted - mean[None, :]
    weighted = anomaly * (measured_precision_factor * live)[None, :]
    gram = jnp.dot(weighted, anomaly.T, precision=lax.Precision.HIGHEST)
    drive = jnp.dot(weighted, measured_reading - mean, precision=lax.Precision.HIGHEST)
    mixing = transform(gram, drive, ensemble_vectors).astype(jnp.float32)
    ensemble_groups = jnp.moveaxis(predicted_grids.reshape(ensemble_vectors, meridional_strips, STRIP_PARALLELS, PHYSICAL_VARS, GRID_MERIDIANS), 1, 0)

    def blend(block):
        return jnp.einsum('jrcl,jk->krcl', block.astype(jnp.float32), mixing).astype(jnp.bfloat16)
    mixed = lax.map(blend, ensemble_groups)
    return jnp.moveaxis(mixed, 0, 1).reshape(ensemble_vectors, GRID_PARALLELS, PHYSICAL_VARS, GRID_MERIDIANS)
```

```python
import functools

import jax
import jax.numpy as jnp
from jax import lax
from jax.experimental import pallas as pl
from jax.experimental.pallas import tpu as pltpu
from jax.sharding import PartitionSpec as P

NS_STEPS = 16
LON = 1440
WIDE = 1536
MAIN = 1408
PACK = 5760
F32 = jnp.float32
BF16 = jnp.bfloat16
ANY = pl.BlockSpec(memory_space=pl.ANY)
VM = pl.BlockSpec(memory_space=pltpu.VMEM)
SM = pl.BlockSpec(memory_space=pltpu.SMEM)


def remote(src, dst, send, recv, peer):
    return pltpu.make_async_remote_copy(
        src_ref=src, dst_ref=dst, send_sem=send, recv_sem=recv, device_id=peer
    )


def widen(x):
    last = jnp.concatenate(
        [x[:, MAIN:LON], x[:, 0:32], x[:, 0:32], x[:, MAIN:LON]], axis=1
    )
    return jnp.concatenate([x[:, :MAIN], last], axis=1)


def conv_rows(src, count, weights, bias, acc_near, acc_far, emit):
    def body(q, carry):
        row = src[q]
        taps = jnp.concatenate(
            [pltpu.roll(row, 1, 1), row, pltpu.roll(row, WIDE - 1, 1)], axis=0
        )
        part = jnp.dot(weights, taps, preferred_element_type=F32)
        total = acc_near[...] + part[128:192]
        acc_near[...] = acc_far[...] + part[64:128]
        acc_far[...] = part[0:64]

        @pl.when(q >= 2)
        def _():
            center = src[q - 1].astype(F32)
            emit(q - 2, (center + jnp.tanh(total + bias)).astype(BF16))

        return carry

    lax.fori_loop(0, count, body, 0)


def forecast_kernel(
    x_ref, w_ref, b_ref, f_ref,
    xin, wide, mid, acc_near, acc_far, rem, fields,
    load_sem, halo_send, halo_recv, start_send, start_recv,
    keep_sem, y_send, y_recv, c_send, c_recv, g_send, g_recv,
):
    g = lax.axis_index("member")
    b = lax.axis_index("band")
    ypeer = {"member": g ^ 2}
    cpeer = {"member": g ^ 1}
    up = {"band": lax.rem(b + 1, 32)}
    down = {"band": lax.rem(b + 31, 32)}
    barrier = pltpu.get_barrier_semaphore()
    for peer in (ypeer, cpeer, up, down):
        pl.semaphore_signal(barrier, inc=1, device_id=peer)

    def load(m):
        return pltpu.make_async_copy(x_ref.at[m], xin.at[m, 2:10], load_sem.at[m])

    for m in (1, 2, 3, 0):
        load(m).start()
    pl.semaphore_wait(barrier, 4)

    def halo_up(slot, src):
        return remote(src, xin.at[slot, 0:2], halo_send.at[slot, 0], halo_recv.at[slot, 0], up)

    def halo_down(slot, src):
        return remote(src, xin.at[slot, 10:12], halo_send.at[slot, 1], halo_recv.at[slot, 1], down)

    def halo_start(slot, high, low):
        @pl.when(b < 31)
        def _():
            halo_up(slot, high).start()

        @pl.when(b > 0)
        def _():
            halo_down(slot, low).start()

    def own_halo(m):
        halo_start(m, x_ref.at[m, 6:8], x_ref.at[m, 0:2])

    def start_copy():
        return remote(x_ref.at[0], xin.at[4, 2:10], start_send, start_recv, ypeer)

    own_halo(1)
    start_copy().start()
    for m in (2, 3, 0):
        own_halo(m)

    weights = w_ref[...]
    bias = b_ref[...]

    def keep(slot, d, m):
        return pltpu.make_async_copy(fields.at[slot], f_ref.at[d, m], keep_sem.at[slot])

    def y_copy(m):
        return remote(f_ref.at[0, m], f_ref.at[2, m], y_send.at[m], y_recv.at[m], ypeer)

    def c_copy(m):
        return remote(f_ref.at[0, m], f_ref.at[1, m], c_send.at[m], c_recv.at[m], cpeer)

    def g_copy(m):
        return remote(f_ref.at[2, m], f_ref.at[3, m], g_send.at[m], g_recv.at[m], cpeer)

    def iteration(i, carry):
        slot = jnp.where(i == 4, 4, lax.rem(i + 1, 4))

        @pl.when(i < 4)
        def _():
            load(slot).wait()

        @pl.when(b > 0)
        def _():
            halo_up(slot, x_ref.at[0, 6:8]).wait_recv()

        @pl.when(b < 31)
        def _():
            halo_down(slot, x_ref.at[0, 0:2]).wait_recv()

        @pl.when(b == 0)
        def _():
            xin[slot, 0:2] = jnp.zeros((2, 64, LON), BF16)

        @pl.when(b == 31)
        def _():
            xin[slot, 10:12] = jnp.zeros((2, 64, LON), BF16)

        def spread(r, c):
            wide[r] = widen(xin[slot, r])
            return c

        lax.fori_loop(0, 12, spread, 0)

        def emit_mid(r, value):
            mid[r] = value

        conv_rows(wide, 12, weights, bias, acc_near, acc_far, emit_mid)

        @pl.when(b == 0)
        def _():
            mid[0] = jnp.zeros((64, WIDE), BF16)

        @pl.when(b == 31)
        def _():
            mid[9] = jnp.zeros((64, WIDE), BF16)

        def emit_field(r, value):
            half = r // 4
            offset = pl.multiple_of(lax.rem(r, 4) * MAIN, 128)
            fields[slot, half, :, pl.ds(offset, MAIN)] = value[:, :MAIN]
            rem[r] = value[:, MAIN:WIDE]

        conv_rows(mid, 10, weights, bias, acc_near, acc_far, emit_field)
        lane = lax.broadcasted_iota(jnp.int32, (64, 128), 1)
        for half in range(2):
            tail = rem[4 * half]
            for j in range(1, 4):
                tail = jnp.where(lane < 32 * j, tail, pltpu.roll(rem[4 * half + j], 32 * j, 1))
            fields[slot, half, :, 4 * MAIN : PACK] = tail

        @pl.when(i < 4)
        def _():
            keep(slot, 0, slot).start()
            keep(slot, 0, slot).wait()
            c_copy(slot).start()

        @pl.when(i < 3)
        def _():
            y_copy(slot).start()

        @pl.when(i == 2)
        def _():
            start_copy().wait_recv()
            halo_start(4, xin.at[4, 8:10], xin.at[4, 2:4])

        @pl.when(i == 4)
        def _():
            keep(4, 2, 0).start()
            keep(4, 2, 0).wait()
            g_copy(0).start()

        return carry

    lax.fori_loop(0, 5, iteration, 0)

    start_copy().wait_send()
    for slot in range(5):
        @pl.when(b < 31)
        def _():
            halo_up(slot, x_ref.at[0, 6:8]).wait_send()

        @pl.when(b > 0)
        def _():
            halo_down(slot, x_ref.at[0, 0:2]).wait_send()

    for m in (1, 2, 3):
        y_copy(m).wait_recv()
        g_copy(m).start()
    for m in (1, 2, 3):
        y_copy(m).wait_send()
    for m in range(4):
        c_copy(m).wait()
        g_copy(m).wait()


def run_forecast(x, weights, bias):
    dma = pltpu.SemaphoreType.DMA
    return pl.pallas_call(
        forecast_kernel,
        out_shape=jax.ShapeDtypeStruct((4, 4, 2, 64, PACK), BF16),
        in_specs=[ANY, VM, VM],
        out_specs=ANY,
        scratch_shapes=[
            pltpu.VMEM((5, 12, 64, LON), BF16),
            pltpu.VMEM((12, 64, WIDE), BF16),
            pltpu.VMEM((10, 64, WIDE), BF16),
            pltpu.VMEM((64, WIDE), F32),
            pltpu.VMEM((64, WIDE), F32),
            pltpu.VMEM((8, 64, 128), BF16),
            pltpu.VMEM((5, 2, 64, PACK), BF16),
            dma((4,)), dma((5, 2)), dma((5, 2)), dma, dma,
            dma((5,)), dma((4,)), dma((4,)), dma((4,)), dma((4,)), dma((4,)), dma((4,)),
        ],
        compiler_params=pltpu.CompilerParams(
            collective_id=1, has_side_effects=True, vmem_limit_bytes=56 << 20
        ),
        name="forecast",
    )(x, weights, bias)


def pick_kernel(index_ref, lane_ref, f_ref, p_ref, fv, wide, slab, sem):
    copy = pltpu.make_async_copy(f_ref.at[0], fv, sem)
    copy.start()
    copy.wait()
    for m in range(4):
        for half in range(2):
            widen_field(fv.at[m, half], wide.at[m], half)
    pick_loop(index_ref, lane_ref, p_ref, wide, slab)


def widen_field(src, dst, half):
    for block in range(45):
        start = block * 128
        dst[start + half * 64 : start + half * 64 + 64, :] = src[:, start : start + 128].astype(F32)


def pick_loop(index_ref, lane_ref, p_ref, wide, slab):
    def group(n, carry):
        base = n * 128

        def fetch(t, c):
            for u in range(8):
                slot = t * 8 + u
                code = index_ref[base + slot]
                for m in range(4):
                    slab[m, pl.ds(slot, 1), :] = wide[m, pl.ds(code, 1), :]
            return c

        lax.fori_loop(0, 16, fetch, 0)
        lanes = lane_ref[pl.ds(pl.multiple_of(base, 128), 128), :]
        hot = lax.broadcasted_iota(jnp.int32, (128, 128), 1) == lanes
        total = jnp.zeros((8, 128), F32)
        rows = lax.broadcasted_iota(jnp.int32, (8, 128), 0)
        for m in range(4):
            masked = jnp.where(hot, slab[m], 0.0).astype(BF16)
            ones = jnp.where(rows == m, 1.0, 0.0).astype(BF16)
            total = total + lax.dot_general(
                ones, masked, (((1,), (1,)), ((), ())), preferred_element_type=F32
            )
        p_ref[:, pl.ds(pl.multiple_of(base, 128), 128)] = total
        return carry

    lax.fori_loop(0, 16, group, 0)


def run_pick(index, lane, fields):
    return pl.pallas_call(
        pick_kernel,
        out_shape=jax.ShapeDtypeStruct((8, 2048), F32),
        in_specs=[SM, VM, ANY],
        out_specs=VM,
        scratch_shapes=[
            pltpu.VMEM((4, 2, 64, PACK), BF16),
            pltpu.VMEM((4, PACK, 128), F32),
            pltpu.VMEM((4, 128, 128), F32),
            pltpu.SemaphoreType.DMA,
        ],
        compiler_params=pltpu.CompilerParams(vmem_limit_bytes=56 << 20),
        name="pick",
    )(index, lane, fields)


def exact(a, b, dims=(((1,), (0,)), ((), ()))):
    return lax.dot_general(
        a, b, dims, precision=lax.Precision.HIGHEST, preferred_element_type=F32
    )


def transform(gram, drive):
    n = 16
    eye = (
        lax.broadcasted_iota(jnp.int32, (n, n), 0) == lax.broadcasted_iota(jnp.int32, (n, n), 1)
    ).astype(F32)
    system = eye + gram / (n - 1.0)
    scale = jnp.sum(jnp.sum(system * eye, axis=1, keepdims=True), axis=0, keepdims=True)
    iterate = system / scale
    root = eye
    for _ in range(NS_STEPS):
        factor = 0.5 * (3.0 * eye - exact(root, iterate))
        iterate = exact(iterate, factor)
        root = exact(factor, root)
    spread = root / jnp.sqrt(scale)
    mean_weights = exact(exact(root, root), drive) / (scale * (n - 1.0))
    centering = eye - 1.0 / n
    return 1.0 / n + exact(centering, mean_weights + spread)


def stats_kernel(
    p_ref, live_ref, reading_ref, precision_ref, k_ref,
    preds, sums, p_send, p_recv, z_send, z_recv, x_send, x_recv, h_send, h_recv,
):
    g = lax.axis_index("member")
    b = lax.axis_index("band")
    z = lax.rem(b, 4)
    xx = lax.rem(b // 4, 4)
    hi = b // 16
    members = [{"member": g ^ d} for d in (1, 2, 3)]
    zs = [{"band": b - z + lax.rem(z + d, 4)} for d in (1, 2, 3)]
    xs = [{"band": hi * 16 + lax.rem(xx + d, 4) * 4 + z} for d in (1, 2, 3)]
    far = {"band": lax.rem(b + 16, 32), "member": g ^ 2}
    barrier = pltpu.get_barrier_semaphore()
    for peer in members + zs + xs + [far]:
        pl.semaphore_signal(barrier, inc=1, device_id=peer)
    pl.semaphore_wait(barrier, 10)

    preds[g] = p_ref[...]
    copies = [
        remote(p_ref, preds.at[g], p_send.at[d], p_recv.at[d], members[d]) for d in range(3)
    ]
    for c in copies:
        c.start()
    for c in copies:
        c.wait()
    predicted = jnp.concatenate([preds[d, 0:4] for d in range(4)], axis=0)
    mean = jnp.sum(predicted, axis=0, keepdims=True) * (1.0 / 16.0)
    anomaly = predicted - mean
    weighted = anomaly * (precision_ref[...] * live_ref[...])
    gram = exact(weighted, anomaly, (((1,), (1,)), ((), ())))
    drive = jnp.sum(weighted * (reading_ref[...] - mean), axis=1, keepdims=True)
    pair = jnp.concatenate([gram, drive, jnp.zeros((16, 111), F32)], axis=1)

    def reduce(stage, place, pair, peers, sends, recvs):
        sums[stage, place] = pair
        copies = [
            remote(sums.at[stage, place], sums.at[stage, place], sends.at[d], recvs.at[d], peer)
            for d, peer in enumerate(peers)
        ]
        for c in copies:
            c.start()
        for c in copies:
            c.wait()

    reduce(0, z, pair, zs, z_send, z_recv)
    pair = (sums[0, 0] + sums[0, 1]) + (sums[0, 2] + sums[0, 3])
    reduce(1, xx, pair, xs, x_send, x_recv)
    pair = (sums[1, 0] + sums[1, 1]) + (sums[1, 2] + sums[1, 3])
    reduce(2, hi, pair, [far], h_send, h_recv)
    pair = sums[2, 0] + sums[2, 1]
    mixing = transform(pair[:, 0:16], pair[:, 16:17]).astype(BF16)
    k_ref[...] = expand(mixing, g)


def expand(mixing, g):
    def iota(shape, dim):
        return lax.broadcasted_iota(jnp.int32, shape, dim)

    own = (iota((64, 16), 1) == 4 * g + iota((64, 16), 0) // 16).astype(BF16)
    column = iota((16, 256), 1)
    source = 4 * jnp.bitwise_xor(column // 64, g) + lax.rem(column // 16, 4)
    order = (iota((16, 256), 0) == source).astype(BF16)
    picked = lax.dot_general(
        own, mixing, (((1,), (1,)), ((), ())), preferred_element_type=F32
    ).astype(BF16)
    full = jnp.dot(picked, order, preferred_element_type=F32)
    same = lax.rem(iota((64, 256), 0), 16) == lax.rem(iota((64, 256), 1), 16)
    return jnp.where(same, full, 0.0).astype(BF16)


def run_stats(predicted, live, reading, precision):
    dma = pltpu.SemaphoreType.DMA
    return pl.pallas_call(
        stats_kernel,
        out_shape=jax.ShapeDtypeStruct((64, 256), BF16),
        in_specs=[VM] * 4,
        out_specs=VM,
        scratch_shapes=[
            pltpu.VMEM((4, 8, 2048), F32),
            pltpu.VMEM((3, 4, 16, 128), F32),
            dma((3,)), dma((3,)), dma((3,)), dma((3,)), dma((3,)), dma((3,)), dma((1,)), dma((1,)),
        ],
        compiler_params=pltpu.CompilerParams(collective_id=2, has_side_effects=True),
        name="stats",
    )(predicted, live, reading, precision)


def mix_kernel(k_ref, f_ref, o_ref):
    mats = k_ref[...]

    def product(lo, width):
        block = f_ref[:, :, 0, :, lo : lo + width].reshape(256, width)
        return jnp.dot(mats, block, preferred_element_type=F32).astype(BF16).reshape(4, 16, width)

    tail = product(4 * MAIN, 128)
    for j in range(4):
        o_ref[:, j, :, 0:MAIN] = product(j * MAIN, MAIN)
        o_ref[:, j, :, MAIN:LON] = tail[:, :, 32 * j : 32 * j + 32]


def run_mix(mats, fields):
    return pl.pallas_call(
        mix_kernel,
        grid=(2, 4),
        out_shape=jax.ShapeDtypeStruct((4, 8, 64, LON), BF16),
        in_specs=[
            pl.BlockSpec((64, 256), lambda h, c: (0, 0)),
            pl.BlockSpec((4, 4, 1, 16, PACK), lambda h, c: (0, 0, h, c, 0)),
        ],
        out_specs=pl.BlockSpec((4, 4, 16, LON), lambda h, c: (0, h, c, 0)),
        compiler_params=pltpu.CompilerParams(vmem_limit_bytes=56 << 20),
        name="mix",
    )(mats, fields)


def local(x, kernel, offset, position, slots, reading, precision):
    weights = jnp.transpose(kernel, (0, 2, 1, 3)).reshape(192, 192)
    fields = run_forecast(x, weights, offset[:, None])
    flat = position // LON
    lon = position - flat * LON
    row = flat // 64
    part = row // 4
    j = row - part * 4
    lane = jnp.where(lon < MAIN, j * MAIN + lon, 4 * MAIN + 32 * j + lon - MAIN)
    index = (lane // 128) * 128 + part * 64 + flat - row * 64
    lane = lax.rem(lane, 128)
    predicted = run_pick(index, lane[:, None], fields)
    live = (lax.broadcasted_iota(jnp.int32, (1, 2048), 1) < slots[0]).astype(F32)
    mats = run_stats(predicted, live, reading[None], precision[None])
    return run_mix(mats, fields)


def solution(mesh):
    return jax.shard_map(
        local,
        mesh=mesh,
        in_specs=(
            P("member", "band", None, None), P(), P(), P("band"), P("band"), P("band"), P("band"),
        ),
        out_specs=P("member", "band", None, None),
        check_vma=False,
    )
```

```python
import functools

import jax
import jax.numpy as jnp
from jax import lax
from jax.experimental import pallas as pl
from jax.experimental.pallas import tpu as pltpu
from jax.sharding import PartitionSpec as P

NS_STEPS = 16
LON = 1440
WIDE = 1536
MAIN = 1408
PACK = 5760
F32 = jnp.float32
BF16 = jnp.bfloat16
ORDER = (1, 2, 3, 0)
YBASE = {1: 1, 2: 2, 3: 6}
ANY = pl.BlockSpec(memory_space=pl.ANY)
VM = pl.BlockSpec(memory_space=pltpu.VMEM)
SM = pl.BlockSpec(memory_space=pltpu.SMEM)


def remote(src, dst, send, recv, peer):
    return pltpu.make_async_remote_copy(
        src_ref=src, dst_ref=dst, send_sem=send, recv_sem=recv, device_id=peer
    )


def widen(x):
    last = jnp.concatenate(
        [x[:, MAIN:LON], x[:, 0:32], x[:, 0:32], x[:, MAIN:LON]], axis=1
    )
    return jnp.concatenate([x[:, :MAIN], last], axis=1)


def conv_rows(src, count, weights, bias, acc_near, acc_far, emit):
    def body(q, carry):
        row = src[q]
        taps = jnp.concatenate(
            [pltpu.roll(row, 1, 1), row, pltpu.roll(row, WIDE - 1, 1)], axis=0
        )
        part = jnp.dot(weights, taps, preferred_element_type=F32)
        total = acc_near[...] + part[128:192]
        acc_near[...] = acc_far[...] + part[64:128]
        acc_far[...] = part[0:64]

        @pl.when(q >= 2)
        def _():
            center = src[q - 1].astype(F32)
            emit(q - 2, (center + jnp.tanh(total + bias)).astype(BF16))

        return carry

    lax.fori_loop(0, count, body, 0)


def forecast_kernel(
    x_ref, kernel_ref, offset_ref, position_ref, slots_ref, reading_ref, precision_ref,
    f_ref, mats_ref,
    xin, wide, mid, acc_near, acc_far, rem, fields, weights_ref, flat, slab, code, code_mem, lanes,
    relay, own_pred, preds, sums,
    load_sem, halo_send, halo_recv, relay_send, relay_recv, start_send, start_recv,
    keep_sem, y_send, y_recv, c_send, c_recv, g_send, g_recv, code_sem,
    p_send, p_recv, z_send, z_recv, s_send, s_recv, h_send, h_recv,
):
    g = lax.axis_index("member")
    b = lax.axis_index("band")
    ypeer = {"member": g ^ 2}
    cpeer = {"member": g ^ 1}
    up = {"band": lax.rem(b + 1, 32)}
    down = {"band": lax.rem(b + 31, 32)}
    z = lax.rem(b, 4)
    xx = lax.rem(b // 4, 4)
    hi = b // 16
    members = [ypeer, cpeer, {"member": g ^ 3}]
    zs = [{"band": b - z + lax.rem(z + d, 4)} for d in (1, 2, 3)]
    xs = [{"band": hi * 16 + lax.rem(xx + d, 4) * 4 + z} for d in (1, 2, 3)]
    far = {"band": lax.rem(b + 16, 32), "member": g ^ 2}
    edge_low = b == 15
    edge_high = b == 16
    edge = jnp.logical_or(edge_low, edge_high)
    relay_up = jnp.logical_and(b >= 23, z == 3)
    relay_down = jnp.logical_and(b <= 8, z == 0)
    relaying = jnp.logical_or(relay_up, relay_down)
    across = {"band": jnp.where(edge_low, 16, 15), "member": g ^ 2}

    barrier = pltpu.get_barrier_semaphore()
    for peer in members + zs + xs + [far, up, down]:
        pl.semaphore_signal(barrier, inc=1, device_id=peer)

    @pl.when(edge)
    def _():
        pl.semaphore_signal(barrier, inc=1, device_id=across)
        for band in (0, 4, 8, 23, 27, 31):
            pl.semaphore_signal(barrier, inc=1, device_id={"band": band})

    @pl.when(relaying)
    def _():
        for band in (15, 16):
            pl.semaphore_signal(barrier, inc=1, device_id={"band": band})

    def load(m):
        return pltpu.make_async_copy(x_ref.at[m], xin.at[m, 2:10], load_sem.at[m])

    for m in ORDER:
        load(m).start()
    pl.semaphore_wait(barrier, 12 + jnp.where(edge, 7, 0) + jnp.where(relaying, 2, 0))

    def halo_up(slot, src, peer=up):
        return remote(src, xin.at[slot, 0:2], halo_send.at[slot, 0], halo_recv.at[slot, 0], peer)

    def halo_down(slot, src, peer=down):
        return remote(src, xin.at[slot, 10:12], halo_send.at[slot, 1], halo_recv.at[slot, 1], peer)

    def to_relay(slot, src, side, band):
        return remote(src, relay, halo_send.at[slot, side], relay_recv, {"band": band})

    def own_halo(n):
        m = ORDER[n]
        high = x_ref.at[m, 6:8]
        low = x_ref.at[m, 0:2]
        plain_up = jnp.logical_and(b < 31, jnp.logical_not(edge_low)) if n else b < 31
        plain_down = jnp.logical_and(b > 0, jnp.logical_not(edge_high)) if n else b > 0

        @pl.when(plain_up)
        def _():
            halo_up(m, high).start()

        @pl.when(plain_down)
        def _():
            halo_down(m, low).start()

        if n:
            @pl.when(edge_low)
            def _():
                to_relay(m, high, 0, 19 + 4 * n).start()

            @pl.when(edge_high)
            def _():
                to_relay(m, low, 1, 12 - 4 * n).start()

    def start_copy():
        return remote(x_ref.at[0], xin.at[4, 2:10], start_send, start_recv, ypeer)

    own_halo(0)
    start_copy().start()
    for n in (1, 2, 3):
        own_halo(n)

    @pl.when(edge_low)
    def _():
        halo_up(4, x_ref.at[0, 6:8], across).start()

    @pl.when(edge_high)
    def _():
        halo_down(4, x_ref.at[0, 0:2], across).start()

    pos = position_ref[...]
    q5 = jnp.right_shift(pos, 5)
    flat_row = jnp.right_shift(q5 * 46604, 21)
    lon = pos - flat_row * LON
    row = jnp.right_shift(flat_row, 6)
    part = jnp.right_shift(row, 2)
    j = row - part * 4
    lane = jnp.where(lon < MAIN, j * MAIN + lon, 4 * MAIN + 32 * j + lon - MAIN)
    block = jnp.right_shift(lane, 7)
    code[...] = block * 128 + part * 64 + flat_row - row * 64
    lanes[...] = lane - block * 128
    to_scalar = pltpu.make_async_copy(code, code_mem, code_sem)
    to_scalar.start()

    for tap in range(3):
        weights_ref[64 * tap : 64 * tap + 64] = jnp.concatenate(
            [kernel_ref[tap, 0], kernel_ref[tap, 1], kernel_ref[tap, 2]], axis=1
        )
    square = (64, 64)
    diagonal = lax.broadcasted_iota(jnp.int32, square, 0) == lax.broadcasted_iota(jnp.int32, square, 1)
    bias = jnp.sum(
        jnp.where(diagonal, jnp.broadcast_to(offset_ref[...], square), 0.0), axis=1, keepdims=True
    )
    to_scalar.wait()

    def relay_copy(n):
        m = ORDER[n]
        return (
            remote(relay, xin.at[m, 0:2], relay_send, halo_recv.at[m, 0], {"band": 16}),
            remote(relay, xin.at[m, 10:12], relay_send, halo_recv.at[m, 1], {"band": 15}),
        )

    @pl.when(relaying)
    def _():
        to_relay(0, x_ref.at[0, 0:2], 0, 0).wait_recv()

    for n in (1, 2, 3):
        @pl.when(b == 19 + 4 * n)
        def _():
            relay_copy(n)[0].start()

        @pl.when(b == 12 - 4 * n)
        def _():
            relay_copy(n)[1].start()

    def keep(slot, d, m):
        return pltpu.make_async_copy(fields.at[slot], f_ref.at[d, m], keep_sem.at[slot])

    def piece(p, count):
        if count == 1:
            return (slice(None),) * 3
        if count == 4:
            return (p // 2, pl.ds(lax.rem(p, 2) * 32, 32), slice(None))
        return (p // 4, pl.ds(lax.rem(p, 4) * 16, 16), slice(None))

    def y_copy(m, p, count):
        at = piece(p, count)
        k = YBASE[m] + p
        return remote(
            fields.at[(m,) + at], f_ref.at[(2, m) + at], y_send.at[k], y_recv.at[k], ypeer
        )

    def g_copy(m, p, count):
        at = piece(p, count)
        k = YBASE[m] + p
        return remote(
            f_ref.at[(2, m) + at], f_ref.at[(3, m) + at], g_send.at[k], g_recv.at[k], cpeer
        )

    def start_g():
        return remote(fields.at[4], f_ref.at[3, 0], g_send.at[0], g_recv.at[0], cpeer)

    def c_copy(m):
        return remote(fields.at[m], f_ref.at[1, m], c_send.at[m], c_recv.at[m], cpeer)

    pred_copies = [
        remote(own_pred, preds.at[g], p_send.at[d], p_recv.at[d], members[d]) for d in range(3)
    ]

    def iteration(i, carry):
        slot = jnp.where(i == 4, 4, lax.rem(i + 1, 4))

        @pl.when(i < 4)
        def _():
            load(slot).wait()

        @pl.when(b > 0)
        def _():
            halo_up(slot, x_ref.at[0, 6:8]).wait_recv()

        @pl.when(b < 31)
        def _():
            halo_down(slot, x_ref.at[0, 0:2]).wait_recv()

        @pl.when(b == 0)
        def _():
            xin[slot, 0:2] = jnp.zeros((2, 64, LON), BF16)

        @pl.when(b == 31)
        def _():
            xin[slot, 10:12] = jnp.zeros((2, 64, LON), BF16)

        def spread(r, c):
            wide[r] = widen(xin[slot, r])
            return c

        lax.fori_loop(0, 12, spread, 0)
        weights = weights_ref[...]

        def emit_mid(r, value):
            mid[r] = value

        conv_rows(wide, 12, weights, bias, acc_near, acc_far, emit_mid)

        @pl.when(b == 0)
        def _():
            mid[0] = jnp.zeros((64, WIDE), BF16)

        @pl.when(b == 31)
        def _():
            mid[9] = jnp.zeros((64, WIDE), BF16)

        def emit_field(r, value):
            half = r // 4
            offset = pl.multiple_of(lax.rem(r, 4) * MAIN, 128)
            fields[slot, half, :, pl.ds(offset, MAIN)] = value[:, :MAIN]
            rem[r] = value[:, MAIN:WIDE]

        conv_rows(mid, 10, weights, bias, acc_near, acc_far, emit_field)
        lane = lax.broadcasted_iota(jnp.int32, (64, 128), 1)
        for half in range(2):
            tail = rem[4 * half]
            for j in range(1, 4):
                tail = jnp.where(lane < 32 * j, tail, pltpu.roll(rem[4 * half + j], 32 * j, 1))
            fields[slot, half, :, 4 * MAIN : PACK] = tail

        @pl.when(i < 4)
        def _():
            keep(slot, 0, slot).start()
            c_copy(slot).start()

        @pl.when(i == 0)
        def _():
            y_copy(1, 0, 1).start()

        @pl.when(i == 1)
        def _():
            for p in range(3):
                y_copy(2, p, 4).start()

        @pl.when(i == 2)
        def _():
            start_copy().wait_recv()

            @pl.when(jnp.logical_and(b < 31, jnp.logical_not(edge_low)))
            def _():
                halo_up(4, xin.at[4, 8:10]).start()

            @pl.when(jnp.logical_and(b > 0, jnp.logical_not(edge_high)))
            def _():
                halo_down(4, xin.at[4, 2:4]).start()

        @pl.when(i < 4)
        def _():
            for half in range(2):
                widen_field(fields.at[slot, half], flat.at[slot], half)

        @pl.when(i == 3)
        def _():
            pick_loop(code_mem, lanes, own_pred, flat, slab)
            for c in pred_copies:
                c.start()
            y_copy(2, 3, 4).start()
            for p in range(8):
                y_copy(3, p, 8).start()
            y_copy(1, 0, 1).wait_recv()
            g_copy(1, 0, 1).start()

        @pl.when(i == 4)
        def _():
            keep(4, 2, 0).start()
            start_g().start()

        return carry

    lax.fori_loop(0, 5, iteration, 0)

    for c in pred_copies:
        c.wait()
    preds[g] = own_pred[...]
    predicted = jnp.concatenate([preds[d, 0:4] for d in range(4)], axis=0)

    def line(ref):
        return jnp.concatenate([ref[n : n + 1] for n in range(16)], axis=1)

    live = (lax.broadcasted_iota(jnp.int32, (1, 2048), 1) < slots_ref[0]).astype(F32)
    mean = jnp.sum(predicted, axis=0, keepdims=True) * (1.0 / 16.0)
    anomaly = predicted - mean
    weighted = anomaly * (line(precision_ref) * live)
    gram = exact(weighted, anomaly, (((1,), (1,)), ((), ())))
    drive = jnp.sum(weighted * (line(reading_ref) - mean), axis=1, keepdims=True)
    pair = jnp.concatenate([gram, drive, jnp.zeros((16, 111), F32)], axis=1)

    def reduce(stage, place, pair, peers, sends, recvs):
        sums[stage, place] = pair
        copies = [
            remote(sums.at[stage, place], sums.at[stage, place], sends.at[d], recvs.at[d], peer)
            for d, peer in enumerate(peers)
        ]
        for c in copies:
            c.start()
        for c in copies:
            c.wait()

    reduce(0, z, pair, zs, z_send, z_recv)
    pair = (sums[0, 0] + sums[0, 1]) + (sums[0, 2] + sums[0, 3])
    reduce(1, xx, pair, xs, s_send, s_recv)
    pair = (sums[1, 0] + sums[1, 1]) + (sums[1, 2] + sums[1, 3])
    reduce(2, hi, pair, [far], h_send, h_recv)
    pair = sums[2, 0] + sums[2, 1]
    mixing = transform(pair[:, 0:16], pair[:, 16:17]).astype(BF16)
    mats_ref[...] = expand(mixing, g)

    for m, count in ((2, 4), (3, 8)):
        def forward(p, carry):
            y_copy(m, p, count).wait_recv()
            g_copy(m, p, count).start()
            return carry

        lax.fori_loop(0, count, forward, 0)

    start_copy().wait_send()
    for slot in range(5):
        keep(slot, 0, 0).wait()

        @pl.when(b < 31)
        def _():
            halo_up(slot, x_ref.at[0, 6:8]).wait_send()

        @pl.when(b > 0)
        def _():
            halo_down(slot, x_ref.at[0, 0:2]).wait_send()

    @pl.when(relaying)
    def _():
        relay_copy(1)[0].wait_send()

    start_g().wait()
    for m, count in ((1, 1), (2, 4), (3, 8)):
        def finish(p, carry):
            y_copy(m, p, count).wait_send()
            g_copy(m, p, count).wait()
            return carry

        lax.fori_loop(0, count, finish, 0)
    for m in range(4):
        c_copy(m).wait()


def run_forecast(x, kernel, offset, position, slots, reading, precision):
    dma = pltpu.SemaphoreType.DMA
    return pl.pallas_call(
        forecast_kernel,
        out_shape=(
            jax.ShapeDtypeStruct((4, 4, 2, 64, PACK), BF16),
            jax.ShapeDtypeStruct((64, 256), BF16),
        ),
        in_specs=[ANY, VM, VM, VM, SM, VM, VM],
        out_specs=(ANY, VM),
        scratch_shapes=[
            pltpu.VMEM((5, 12, 64, LON), BF16),
            pltpu.VMEM((12, 64, WIDE), BF16),
            pltpu.VMEM((10, 64, WIDE), BF16),
            pltpu.VMEM((64, WIDE), F32),
            pltpu.VMEM((64, WIDE), F32),
            pltpu.VMEM((8, 64, 128), BF16),
            pltpu.VMEM((5, 2, 64, PACK), BF16),
            pltpu.VMEM((192, 192), BF16),
            pltpu.VMEM((4, PACK, 128), F32),
            pltpu.VMEM((4, 128, 128), F32),
            pltpu.VMEM((16, 128), jnp.int32),
            pltpu.SMEM((16, 128), jnp.int32),
            pltpu.VMEM((16, 128), jnp.int32),
            pltpu.VMEM((2, 64, LON), BF16),
            pltpu.VMEM((8, 2048), F32),
            pltpu.VMEM((4, 8, 2048), F32),
            pltpu.VMEM((3, 4, 16, 128), F32),
            dma((4,)), dma((5, 2)), dma((5, 2)), dma, dma, dma, dma,
            dma((5,)), dma((14,)), dma((14,)), dma((4,)), dma((4,)), dma((14,)), dma((14,)), dma,
            dma((3,)), dma((3,)), dma((3,)), dma((3,)), dma((3,)), dma((3,)), dma((1,)), dma((1,)),
        ],
        compiler_params=pltpu.CompilerParams(
            collective_id=1, has_side_effects=True, vmem_limit_bytes=58 << 20
        ),
        name="forecast",
    )(x, kernel, offset, position, slots, reading, precision)


def widen_field(src, dst, half):
    for block in range(45):
        start = block * 128
        dst[start + half * 64 : start + half * 64 + 64, :] = src[:, start : start + 128].astype(F32)


def pick_loop(code_mem, lanes, p_ref, flat, slab):
    square = (128, 128)
    down = lax.broadcasted_iota(jnp.int32, square, 0)
    diagonal = down == lax.broadcasted_iota(jnp.int32, square, 1)

    def group(n, carry):
        def fetch(t, c):
            for u in range(8):
                slot = t * 8 + u
                place = code_mem[n, slot]
                for m in range(4):
                    slab[m, pl.ds(slot, 1), :] = flat[m, pl.ds(place, 1), :]
            return c

        lax.fori_loop(0, 16, fetch, 0)
        hot = jnp.where(down == lanes[pl.ds(n, 1), :], 1.0, 0.0).astype(BF16)
        picked = []
        for m in range(4):
            table = jnp.dot(slab[m].astype(BF16), hot, preferred_element_type=F32)
            picked.append(jnp.sum(jnp.where(diagonal, table, 0.0), axis=0, keepdims=True))
        picked.append(jnp.zeros((4, 128), F32))
        p_ref[:, pl.ds(pl.multiple_of(n * 128, 128), 128)] = jnp.concatenate(picked, axis=0)
        return carry

    lax.fori_loop(0, 16, group, 0)


def exact(a, b, dims=(((1,), (0,)), ((), ()))):
    return lax.dot_general(
        a, b, dims, precision=lax.Precision.HIGHEST, preferred_element_type=F32
    )


def transform(gram, drive):
    n = 16
    eye = (
        lax.broadcasted_iota(jnp.int32, (n, n), 0) == lax.broadcasted_iota(jnp.int32, (n, n), 1)
    ).astype(F32)
    system = eye + gram / (n - 1.0)
    scale = jnp.sum(jnp.sum(system * eye, axis=1, keepdims=True), axis=0, keepdims=True)
    iterate = system / scale
    root = eye
    for _ in range(NS_STEPS):
        factor = 0.5 * (3.0 * eye - exact(root, iterate))
        iterate = exact(iterate, factor)
        root = exact(factor, root)
    spread = root / jnp.sqrt(scale)
    mean_weights = exact(exact(root, root), drive) / (scale * (n - 1.0))
    centering = eye - 1.0 / n
    return 1.0 / n + exact(centering, mean_weights + spread)


def expand(mixing, g):
    def iota(shape, dim):
        return lax.broadcasted_iota(jnp.int32, shape, dim)

    own = (iota((64, 16), 1) == 4 * g + iota((64, 16), 0) // 16).astype(BF16)
    column = iota((16, 256), 1)
    source = 4 * jnp.bitwise_xor(column // 64, g) + lax.rem(column // 16, 4)
    order = (iota((16, 256), 0) == source).astype(BF16)
    picked = lax.dot_general(
        own, mixing, (((1,), (1,)), ((), ())), preferred_element_type=F32
    ).astype(BF16)
    full = jnp.dot(picked, order, preferred_element_type=F32)
    same = lax.rem(iota((64, 256), 0), 16) == lax.rem(iota((64, 256), 1), 16)
    return jnp.where(same, full, 0.0).astype(BF16)


def mix_kernel(k_ref, f_ref, o_ref):
    mats = k_ref[...]

    def product(lo, width):
        block = f_ref[:, :, 0, :, lo : lo + width].reshape(256, width)
        return jnp.dot(mats, block, preferred_element_type=F32).astype(BF16).reshape(4, 16, width)

    tail = product(4 * MAIN, 128)
    for j in range(4):
        o_ref[:, j, :, 0:MAIN] = product(j * MAIN, MAIN)
        o_ref[:, j, :, MAIN:LON] = tail[:, :, 32 * j : 32 * j + 32]


def run_mix(mats, fields):
    return pl.pallas_call(
        mix_kernel,
        grid=(2, 4),
        out_shape=jax.ShapeDtypeStruct((4, 8, 64, LON), BF16),
        in_specs=[
            pl.BlockSpec((64, 256), lambda h, c: (0, 0)),
            pl.BlockSpec((4, 4, 1, 16, PACK), lambda h, c: (0, 0, h, c, 0)),
        ],
        out_specs=pl.BlockSpec((4, 4, 16, LON), lambda h, c: (0, h, c, 0)),
        compiler_params=pltpu.CompilerParams(vmem_limit_bytes=56 << 20),
        name="mix",
    )(mats, fields)


def local(x, kernel, offset, position, slots, reading, precision):
    fields, mats = run_forecast(
        x,
        kernel,
        offset.reshape(1, 64),
        position.reshape(16, 128),
        slots,
        reading.reshape(16, 128),
        precision.reshape(16, 128),
    )
    return run_mix(mats, fields)


def solution(mesh):
    return jax.shard_map(
        local,
        mesh=mesh,
        in_specs=(
            P("member", "band", None, None), P(), P(), P("band"), P("band"), P("band"), P("band"),
        ),
        out_specs=P("member", "band", None, None),
        check_vma=False,
    )
```

```python
import functools

import jax
import jax.numpy as jnp
from jax import lax
from jax.experimental import pallas as pl
from jax.experimental.pallas import tpu as pltpu
from jax.sharding import PartitionSpec as P

NS_STEPS = 16
LON = 1440
WIDE = 1536
MAIN = 1408
PACK = 5760
F32 = jnp.float32
BF16 = jnp.bfloat16
ORDER = (1, 2, 3, 0)
YBASE = {1: 1, 2: 2, 3: 6}
RELAYS = (
    (23, 0, 1), (27, 0, 2), (21, 0, 3), (22, 0, 4), (31, 0, 5),
    (8, 1, 1), (4, 1, 2), (10, 1, 3), (9, 1, 4), (0, 1, 5),
)
ANY = pl.BlockSpec(memory_space=pl.ANY)
VM = pl.BlockSpec(memory_space=pltpu.VMEM)
SM = pl.BlockSpec(memory_space=pltpu.SMEM)


def remote(src, dst, send, recv, peer):
    return pltpu.make_async_remote_copy(
        src_ref=src, dst_ref=dst, send_sem=send, recv_sem=recv, device_id=peer
    )


def widen(x):
    last = jnp.concatenate(
        [x[:, MAIN:LON], x[:, 0:32], x[:, 0:32], x[:, MAIN:LON]], axis=1
    )
    return jnp.concatenate([x[:, :MAIN], last], axis=1)


def conv_rows(src, count, weights, bias, acc_near, acc_far, emit):
    def body(q, carry):
        row = src[q]
        taps = jnp.concatenate(
            [pltpu.roll(row, 1, 1), row, pltpu.roll(row, WIDE - 1, 1)], axis=0
        )
        part = jnp.dot(weights, taps, preferred_element_type=F32)
        total = acc_near[...] + part[128:192]
        acc_near[...] = acc_far[...] + part[64:128]
        acc_far[...] = part[0:64]

        @pl.when(q >= 2)
        def _():
            center = src[q - 1].astype(F32)
            emit(q - 2, (center + jnp.tanh(total + bias)).astype(BF16))

        return carry

    lax.fori_loop(0, count, body, 0)


def forecast_kernel(
    x_ref, kernel_ref, offset_ref, position_ref, slots_ref, reading_ref, precision_ref,
    part_ref, last_ref, mats_ref,
    xin, wide, mid, acc_near, acc_far, rem, fields, weights_ref, flat, slab, code, code_mem, lanes,
    relay, own_pred, preds, sums, staged,
    load_sem, halo_send, halo_recv, relay_send, relay_recv, start_send, start_recv,
    last_sem, store_sem, y_send, y_recv, c_send, c_recv, g_send, g_recv, code_sem,
    p_send, p_recv, z_send, z_recv, s_send, s_recv, h_send, h_recv,
):
    g = lax.axis_index("member")
    b = lax.axis_index("band")
    ypeer = {"member": g ^ 2}
    cpeer = {"member": g ^ 1}
    up = {"band": lax.rem(b + 1, 32)}
    down = {"band": lax.rem(b + 31, 32)}
    z = lax.rem(b, 4)
    xx = lax.rem(b // 4, 4)
    hi = b // 16
    members = [ypeer, cpeer, {"member": g ^ 3}]
    zs = [{"band": b - z + lax.rem(z + d, 4)} for d in (1, 2, 3)]
    xs = [{"band": hi * 16 + lax.rem(xx + d, 4) * 4 + z} for d in (1, 2, 3)]
    far = {"band": lax.rem(b + 16, 32), "member": g ^ 2}
    edge_low = b == 15
    edge_high = b == 16
    edge = jnp.logical_or(edge_low, edge_high)
    relaying = functools.reduce(jnp.logical_or, [b == band for band, _, _ in RELAYS])
    across = {"band": jnp.where(edge_low, 16, 15), "member": g ^ 2}

    barrier = pltpu.get_barrier_semaphore()
    for peer in members + zs + xs + [far, up, down]:
        pl.semaphore_signal(barrier, inc=1, device_id=peer)

    @pl.when(edge)
    def _():
        pl.semaphore_signal(barrier, inc=1, device_id=across)
        for band, _, k in RELAYS:
            pl.semaphore_signal(
                barrier, inc=1, device_id={"band": band, "member": g ^ 2 if k > 2 else g}
            )

    for band, _, k in RELAYS:
        @pl.when(b == band)
        def _():
            for target in (15, 16):
                pl.semaphore_signal(
                    barrier, inc=1, device_id={"band": target, "member": g ^ 2 if k > 2 else g}
                )

    def load(m):
        return pltpu.make_async_copy(x_ref.at[m], xin.at[m, 2:10], load_sem.at[m])

    for m in ORDER:
        load(m).start()
    pl.semaphore_wait(barrier, 12 + jnp.where(edge, 11, 0) + jnp.where(relaying, 2, 0))

    def halo_up(slot, src, peer=up):
        return remote(src, xin.at[slot, 0:2], halo_send.at[slot, 0], halo_recv.at[slot, 0], peer)

    def halo_down(slot, src, peer=down):
        return remote(src, xin.at[slot, 10:12], halo_send.at[slot, 1], halo_recv.at[slot, 1], peer)

    def to_relay(slot, src, side, k):
        band = next(band for band, s, n in RELAYS if (s, n) == (side, k))
        peer = {"band": band, "member": g ^ 2 if k > 2 else g}
        return remote(src, relay, halo_send.at[slot, side], relay_recv, peer)

    def edge_rows(n):
        m = ORDER[n]
        for r in range(2):
            k = 2 * n + r
            for side, is_edge, source, row, peer in (
                (0, edge_low, 6 + r, r, up), (1, edge_high, r, 10 + r, down),
            ):
                @pl.when(is_edge)
                def _():
                    src = x_ref.at[m, source : source + 1]
                    if k:
                        to_relay(m, src, side, k).start()
                    else:
                        remote(
                            src, xin.at[m, row : row + 1],
                            halo_send.at[m, side], halo_recv.at[m, side], peer,
                        ).start()

    not_low = jnp.logical_and(b < 31, jnp.logical_not(edge_low))
    not_high = jnp.logical_and(b > 0, jnp.logical_not(edge_high))

    def own_halo(n):
        m = ORDER[n]

        @pl.when(not_low)
        def _():
            halo_up(m, x_ref.at[m, 6:8]).start()

        @pl.when(not_high)
        def _():
            halo_down(m, x_ref.at[m, 0:2]).start()

        if n < 3:
            edge_rows(n)

    def start_copy():
        return remote(x_ref.at[0], xin.at[4, 2:10], start_send, start_recv, ypeer)

    own_halo(0)
    start_copy().start()
    for n in (1, 2, 3):
        own_halo(n)

    @pl.when(edge_low)
    def _():
        halo_up(4, x_ref.at[0, 6:8], across).start()

    @pl.when(edge_high)
    def _():
        halo_down(4, x_ref.at[0, 0:2], across).start()

    pos = position_ref[...]
    q5 = jnp.right_shift(pos, 5)
    flat_row = jnp.right_shift(q5 * 46604, 21)
    lon = pos - flat_row * LON
    row = jnp.right_shift(flat_row, 6)
    part = jnp.right_shift(row, 2)
    j = row - part * 4
    lane = jnp.where(lon < MAIN, j * MAIN + lon, 4 * MAIN + 32 * j + lon - MAIN)
    block = jnp.right_shift(lane, 7)
    code[...] = block * 128 + part * 64 + flat_row - row * 64
    lanes[...] = lane - block * 128
    to_scalar = pltpu.make_async_copy(code, code_mem, code_sem)
    to_scalar.start()

    for tap in range(3):
        weights_ref[64 * tap : 64 * tap + 64] = jnp.concatenate(
            [kernel_ref[tap, 0], kernel_ref[tap, 1], kernel_ref[tap, 2]], axis=1
        )
    square = (64, 64)
    diagonal = lax.broadcasted_iota(jnp.int32, square, 0) == lax.broadcasted_iota(jnp.int32, square, 1)
    bias = jnp.sum(
        jnp.where(diagonal, jnp.broadcast_to(offset_ref[...], square), 0.0), axis=1, keepdims=True
    )
    to_scalar.wait()

    def relay_copy(side, k):
        m = ORDER[k // 2]
        row = (0 if side == 0 else 10) + k % 2
        peer = {"band": 16 if side == 0 else 15, "member": g ^ 2 if k > 2 else g}
        return remote(relay, xin.at[m, row : row + 1], relay_send, halo_recv.at[m, side], peer)

    def relay_now(ks):
        for band, side, k in RELAYS:
            if k in ks:
                @pl.when(b == band)
                def _():
                    remote(x_ref.at[0, 0:1], relay, relay_send, relay_recv, up).wait_recv()
                    relay_copy(side, k).start()

    relay_now((1,))

    def piece(p, count):
        if count == 1:
            return (slice(None),) * 3
        if count == 4:
            return (p // 2, pl.ds(lax.rem(p, 2) * 32, 32), slice(None))
        return (p // 4, pl.ds(lax.rem(p, 4) * 16, 16), slice(None))

    def y_copy(m, p, count):
        at = piece(p, count)
        k = YBASE[m] + p
        return remote(
            fields.at[(0, m) + at], fields.at[(2, m) + at], y_send.at[k], y_recv.at[k], ypeer
        )

    def g_copy(m, p, count):
        at = piece(p, count)
        k = YBASE[m] + p
        return remote(
            fields.at[(2, m) + at], fields.at[(3, m) + at], g_send.at[k], g_recv.at[k], cpeer
        )

    def start_g():
        return remote(fields.at[2, 0], fields.at[3, 0], g_send.at[0], g_recv.at[0], cpeer)

    def c_copy(m):
        return remote(fields.at[0, m], fields.at[1, m], c_send.at[m], c_recv.at[m], cpeer)

    pred_copies = [
        remote(own_pred, preds.at[g], p_send.at[d], p_recv.at[d], members[d]) for d in range(3)
    ]

    def iteration(i, carry):
        slot = jnp.where(i == 4, 4, lax.rem(i + 1, 4))
        home = jnp.where(i == 4, 2, 0)
        own = lax.rem(slot, 4)

        @pl.when(i < 4)
        def _():
            load(slot).wait()

        @pl.when(b > 0)
        def _():
            halo_up(slot, x_ref.at[0, 6:8]).wait_recv()

        @pl.when(b < 31)
        def _():
            halo_down(slot, x_ref.at[0, 0:2]).wait_recv()

        @pl.when(b == 0)
        def _():
            xin[slot, 0:2] = jnp.zeros((2, 64, LON), BF16)

        @pl.when(b == 31)
        def _():
            xin[slot, 10:12] = jnp.zeros((2, 64, LON), BF16)

        def spread(r, c):
            wide[r] = widen(xin[slot, r])
            return c

        lax.fori_loop(0, 12, spread, 0)
        weights = weights_ref[...]

        def emit_mid(r, value):
            mid[r] = value

        conv_rows(wide, 12, weights, bias, acc_near, acc_far, emit_mid)

        @pl.when(b == 0)
        def _():
            mid[0] = jnp.zeros((64, WIDE), BF16)

        @pl.when(b == 31)
        def _():
            mid[9] = jnp.zeros((64, WIDE), BF16)

        def emit_field(r, value):
            half = r // 4
            offset = pl.multiple_of(lax.rem(r, 4) * MAIN, 128)
            fields[home, own, half, :, pl.ds(offset, MAIN)] = value[:, :MAIN]
            rem[r] = value[:, MAIN:WIDE]

        conv_rows(mid, 10, weights, bias, acc_near, acc_far, emit_field)
        lane = lax.broadcasted_iota(jnp.int32, (64, 128), 1)
        for half in range(2):
            tail = rem[4 * half]
            for j in range(1, 4):
                tail = jnp.where(lane < 32 * j, tail, pltpu.roll(rem[4 * half + j], 32 * j, 1))
            fields[home, own, half, :, 4 * MAIN : PACK] = tail

        @pl.when(i < 4)
        def _():
            c_copy(slot).start()

        @pl.when(i == 0)
        def _():
            y_copy(1, 0, 1).start()

            relay_now((2, 3))

        @pl.when(i == 1)
        def _():
            for p in range(2):
                y_copy(2, p, 4).start()
            relay_now((4, 5))
            start_copy().wait_recv()

            @pl.when(not_low)
            def _():
                halo_up(4, xin.at[4, 8:10]).start()

            @pl.when(not_high)
            def _():
                halo_down(4, xin.at[4, 2:4]).start()

            @pl.when(edge_low)
            def _():
                halo_up(0, xin.at[4, 8:10], across).start()

            @pl.when(edge_high)
            def _():
                halo_down(0, xin.at[4, 2:4], across).start()

        @pl.when(i < 4)
        def _():
            for half in range(2):
                widen_field(fields.at[0, slot, half], flat.at[slot], half)

        @pl.when(i == 3)
        def _():
            pick_loop(code_mem, lanes, own_pred, flat, slab)
            for c in pred_copies:
                c.start()
            y_copy(2, 2, 4).start()
            y_copy(2, 3, 4).start()
            for p in range(8):
                y_copy(3, p, 8).start()
            y_copy(1, 0, 1).wait_recv()
            g_copy(1, 0, 1).start()

        @pl.when(i == 4)
        def _():
            start_g().start()

        return carry

    lax.fori_loop(0, 5, iteration, 0)

    for c in pred_copies:
        c.wait()
    preds[g] = own_pred[...]
    predicted = jnp.concatenate([preds[d, 0:4] for d in range(4)], axis=0)

    def line(ref):
        return jnp.concatenate([ref[n : n + 1] for n in range(16)], axis=1)

    live = (lax.broadcasted_iota(jnp.int32, (1, 2048), 1) < slots_ref[0]).astype(F32)
    mean = jnp.sum(predicted, axis=0, keepdims=True) * (1.0 / 16.0)
    anomaly = predicted - mean
    weighted = anomaly * (line(precision_ref) * live)
    gram = exact(weighted, anomaly, (((1,), (1,)), ((), ())))
    drive = jnp.sum(weighted * (line(reading_ref) - mean), axis=1, keepdims=True)
    pair = jnp.concatenate([gram, drive, jnp.zeros((16, 111), F32)], axis=1)

    def reduce(stage, place, pair, peers, sends, recvs):
        sums[stage, place] = pair
        copies = [
            remote(sums.at[stage, place], sums.at[stage, place], sends.at[d], recvs.at[d], peer)
            for d, peer in enumerate(peers)
        ]
        for c in copies:
            c.start()
        for c in copies:
            c.wait()

    reduce(0, z, pair, zs, z_send, z_recv)
    pair = (sums[0, 0] + sums[0, 1]) + (sums[0, 2] + sums[0, 3])
    reduce(1, xx, pair, xs, s_send, s_recv)
    pair = (sums[1, 0] + sums[1, 1]) + (sums[1, 2] + sums[1, 3])
    reduce(2, hi, pair, [far], h_send, h_recv)
    pair = sums[2, 0] + sums[2, 1]
    mixing = transform(pair[:, 0:16], pair[:, 16:17]).astype(BF16)
    mats_ref[...] = expand(mixing, g)

    mats = mats_ref[...]

    def store(p):
        out = part_ref.at[:, pl.ds(p // 4 * 4, 4), pl.ds(lax.rem(p, 4) * 16, 16), :]
        return pltpu.make_async_copy(
            staged.at[lax.rem(p, 2)], out, store_sem.at[lax.rem(p, 2)]
        )

    def mix(p):
        half = p // 4
        rows = pl.ds(pl.multiple_of(lax.rem(p, 4) * 16, 16), 16)

        def product(lo, width):
            block = fields[:, :, half, rows, lo : lo + width].reshape(256, width)
            out = jnp.dot(mats, block, preferred_element_type=F32)
            return out.astype(BF16).reshape(4, 16, width)

        side = lax.rem(p, 2)
        tail = product(4 * MAIN, 128)
        for j in range(4):
            staged[side, :, j, :, 0:MAIN] = product(j * MAIN, MAIN)
            staged[side, :, j, :, MAIN:LON] = tail[:, :, 32 * j : 32 * j + 32]
        store(p).start()

    def forward(m, count):
        def body(p, carry):
            y_copy(m, p, count).wait_recv()
            g_copy(m, p, count).start()
            return carry

        lax.fori_loop(0, count, body, 0)

    forward(2, 4)
    g_copy(1, 0, 1).wait_recv()
    start_g().wait_recv()
    for m in range(4):
        c_copy(m).wait_recv()

    def last_copy(d, m):
        return pltpu.make_async_copy(
            fields.at[d, m, 1, 48:64], last_ref.at[d, m], last_sem.at[4 * d + m]
        )

    def early(p, carry):
        g_copy(2, p, 4).wait_recv()
        return carry

    lax.fori_loop(0, 4, early, 0)
    for d in range(4):
        for m in range(4):
            if d < 2 or m < 3:
                last_copy(d, m).start()

    def blend(p, carry):
        y_copy(3, p, 8).wait_recv()
        g_copy(3, p, 8).start()

        @pl.when(p > 0)
        def _():
            g_copy(3, p - 1, 8).wait_recv()

            @pl.when(p > 2)
            def _():
                store(p - 3).wait()

            mix(p - 1)

        return carry

    lax.fori_loop(0, 8, blend, 0)
    last_copy(2, 3).start()
    g_copy(3, 7, 8).wait_recv()
    last_copy(3, 3).start()
    store(5).wait()
    store(6).wait()
    for d in range(4):
        for m in range(4):
            last_copy(d, m).wait()

    start_copy().wait_send()
    for slot in range(5):
        @pl.when(b < 31)
        def _():
            halo_up(slot, x_ref.at[0, 6:8]).wait_send()

        @pl.when(b > 0)
        def _():
            halo_down(slot, x_ref.at[0, 0:2]).wait_send()

    @pl.when(relaying)
    def _():
        relay_copy(0, 1).wait_send()

    start_g().wait_send()
    for m, count in ((1, 1), (2, 4), (3, 8)):
        def finish(p, carry):
            y_copy(m, p, count).wait_send()
            g_copy(m, p, count).wait_send()
            return carry

        lax.fori_loop(0, count, finish, 0)
    for m in range(4):
        c_copy(m).wait_send()


def run_forecast(x, kernel, offset, position, slots, reading, precision):
    dma = pltpu.SemaphoreType.DMA
    return pl.pallas_call(
        forecast_kernel,
        out_shape=(
            jax.ShapeDtypeStruct((4, 8, 64, LON), BF16),
            jax.ShapeDtypeStruct((4, 4, 16, PACK), BF16),
            jax.ShapeDtypeStruct((64, 256), BF16),
        ),
        in_specs=[ANY, VM, VM, VM, SM, VM, VM],
        out_specs=(ANY, ANY, VM),
        scratch_shapes=[
            pltpu.VMEM((5, 12, 64, LON), BF16),
            pltpu.VMEM((12, 64, WIDE), BF16),
            pltpu.VMEM((10, 64, WIDE), BF16),
            pltpu.VMEM((64, WIDE), F32),
            pltpu.VMEM((64, WIDE), F32),
            pltpu.VMEM((8, 64, 128), BF16),
            pltpu.VMEM((4, 4, 2, 64, PACK), BF16),
            pltpu.VMEM((192, 192), BF16),
            pltpu.VMEM((4, PACK, 128), F32),
            pltpu.VMEM((4, 128, 128), F32),
            pltpu.VMEM((16, 128), jnp.int32),
            pltpu.SMEM((16, 128), jnp.int32),
            pltpu.VMEM((16, 128), jnp.int32),
            pltpu.VMEM((1, 64, LON), BF16),
            pltpu.VMEM((8, 2048), F32),
            pltpu.VMEM((4, 8, 2048), F32),
            pltpu.VMEM((3, 4, 16, 128), F32),
            pltpu.VMEM((2, 4, 4, 16, LON), BF16),
            dma((4,)), dma((5, 2)), dma((5, 2)), dma, dma, dma, dma,
            dma((16,)), dma((2,)), dma((14,)), dma((14,)), dma((4,)), dma((4,)), dma((14,)), dma((14,)), dma,
            dma((3,)), dma((3,)), dma((3,)), dma((3,)), dma((3,)), dma((3,)), dma((1,)), dma((1,)),
        ],
        compiler_params=pltpu.CompilerParams(
            collective_id=1, has_side_effects=True, vmem_limit_bytes=58 << 20
        ),
        name="forecast",
    )(x, kernel, offset, position, slots, reading, precision)


def widen_field(src, dst, half):
    for block in range(45):
        start = block * 128
        dst[start + half * 64 : start + half * 64 + 64, :] = src[:, start : start + 128].astype(F32)


def pick_loop(code_mem, lanes, p_ref, flat, slab):
    square = (128, 128)
    down = lax.broadcasted_iota(jnp.int32, square, 0)
    diagonal = down == lax.broadcasted_iota(jnp.int32, square, 1)

    def group(n, carry):
        def fetch(t, c):
            for u in range(8):
                slot = t * 8 + u
                place = code_mem[n, slot]
                for m in range(4):
                    slab[m, pl.ds(slot, 1), :] = flat[m, pl.ds(place, 1), :]
            return c

        lax.fori_loop(0, 16, fetch, 0)
        hot = jnp.where(down == lanes[pl.ds(n, 1), :], 1.0, 0.0).astype(BF16)
        picked = []
        for m in range(4):
            table = jnp.dot(slab[m].astype(BF16), hot, preferred_element_type=F32)
            picked.append(jnp.sum(jnp.where(diagonal, table, 0.0), axis=0, keepdims=True))
        picked.append(jnp.zeros((4, 128), F32))
        p_ref[:, pl.ds(pl.multiple_of(n * 128, 128), 128)] = jnp.concatenate(picked, axis=0)
        return carry

    lax.fori_loop(0, 16, group, 0)


def exact(a, b, dims=(((1,), (0,)), ((), ()))):
    return lax.dot_general(
        a, b, dims, precision=lax.Precision.HIGHEST, preferred_element_type=F32
    )


def transform(gram, drive):
    n = 16
    eye = (
        lax.broadcasted_iota(jnp.int32, (n, n), 0) == lax.broadcasted_iota(jnp.int32, (n, n), 1)
    ).astype(F32)
    system = eye + gram / (n - 1.0)
    scale = jnp.sum(jnp.sum(system * eye, axis=1, keepdims=True), axis=0, keepdims=True)
    iterate = system / scale
    root = eye
    for _ in range(NS_STEPS):
        factor = 0.5 * (3.0 * eye - exact(root, iterate))
        iterate = exact(iterate, factor)
        root = exact(factor, root)
    spread = root / jnp.sqrt(scale)
    mean_weights = exact(exact(root, root), drive) / (scale * (n - 1.0))
    centering = eye - 1.0 / n
    return 1.0 / n + exact(centering, mean_weights + spread)


def expand(mixing, g):
    def iota(shape, dim):
        return lax.broadcasted_iota(jnp.int32, shape, dim)

    own = (iota((64, 16), 1) == 4 * g + iota((64, 16), 0) // 16).astype(BF16)
    column = iota((16, 256), 1)
    source = 4 * jnp.bitwise_xor(column // 64, g) + lax.rem(column // 16, 4)
    order = (iota((16, 256), 0) == source).astype(BF16)
    picked = lax.dot_general(
        own, mixing, (((1,), (1,)), ((), ())), preferred_element_type=F32
    ).astype(BF16)
    full = jnp.dot(picked, order, preferred_element_type=F32)
    same = lax.rem(iota((64, 256), 0), 16) == lax.rem(iota((64, 256), 1), 16)
    return jnp.where(same, full, 0.0).astype(BF16)


def finish_kernel(k_ref, last_ref, part_ref, o_ref):
    step = pl.program_id(0)
    mats = k_ref[...]

    @pl.when(step < 3)
    def _():
        o_ref[...] = part_ref[...]

    @pl.when(step == 3)
    def _():
        o_ref[:, :, 0:16] = part_ref[:, :, 0:16]

        def product(lo, width):
            block = last_ref[:, :, :, lo : lo + width].reshape(256, width)
            out = jnp.dot(mats, block, preferred_element_type=F32)
            return out.astype(BF16).reshape(4, 16, width)

        tail = product(4 * MAIN, 128)
        for j in range(4):
            o_ref[:, j, 16:32, 0:MAIN] = product(j * MAIN, MAIN)
            o_ref[:, j, 16:32, MAIN:LON] = tail[:, :, 32 * j : 32 * j + 32]


def run_finish(mats, last, part):
    return pl.pallas_call(
        finish_kernel,
        grid=(4,),
        out_shape=jax.ShapeDtypeStruct((4, 8, 64, LON), BF16),
        in_specs=[
            pl.BlockSpec((64, 256), lambda i: (0, 0)),
            pl.BlockSpec((4, 4, 16, PACK), lambda i: (0, 0, 0, 0)),
            pl.BlockSpec((4, 4, 32, LON), lambda i: (0, i // 2, i % 2, 0)),
        ],
        out_specs=pl.BlockSpec((4, 4, 32, LON), lambda i: (0, i // 2, i % 2, 0)),
        compiler_params=pltpu.CompilerParams(vmem_limit_bytes=60 << 20),
        name="finish",
    )(mats, last, part)


def local(x, kernel, offset, position, slots, reading, precision):
    part, last, mats = run_forecast(
        x,
        kernel,
        offset.reshape(1, 64),
        position.reshape(16, 128),
        slots,
        reading.reshape(16, 128),
        precision.reshape(16, 128),
    )
    return run_finish(mats, last, part)


def solution(mesh):
    return jax.shard_map(
        local,
        mesh=mesh,
        in_specs=(
            P("member", "band", None, None), P(), P(), P("band"), P("band"), P("band"), P("band"),
        ),
        out_specs=P("member", "band", None, None),
        check_vma=False,
    )
```

```python
import functools

import jax
import jax.numpy as jnp
from jax import lax
from jax.experimental import pallas as pl
from jax.experimental.pallas import tpu as pltpu
from jax.sharding import PartitionSpec as P

NS_STEPS = 16
LON = 1440
WIDE = 1536
MAIN = 1408
PACK = 5760
F32 = jnp.float32
BF16 = jnp.bfloat16
ORDER = (1, 2, 3, 0)
YBASE = {1: 1, 2: 2, 3: 6}
RELAYS = (
    (23, 0, 1), (27, 0, 2), (21, 0, 3), (22, 0, 4), (31, 0, 5),
    (8, 1, 1), (4, 1, 2), (10, 1, 3), (9, 1, 4), (0, 1, 5),
)
ANY = pl.BlockSpec(memory_space=pl.ANY)
VM = pl.BlockSpec(memory_space=pltpu.VMEM)
SM = pl.BlockSpec(memory_space=pltpu.SMEM)


def remote(src, dst, send, recv, peer):
    return pltpu.make_async_remote_copy(
        src_ref=src, dst_ref=dst, send_sem=send, recv_sem=recv, device_id=peer
    )


def widen(x):
    last = jnp.concatenate(
        [x[:, MAIN:LON], x[:, 0:32], x[:, 0:32], x[:, MAIN:LON]], axis=1
    )
    return jnp.concatenate([x[:, :MAIN], last], axis=1)


def conv_rows(src, count, weights, bias, acc_near, acc_far, emit):
    def body(q, carry):
        row = src[q]
        taps = jnp.concatenate(
            [pltpu.roll(row, 1, 1), row, pltpu.roll(row, WIDE - 1, 1)], axis=0
        )
        part = jnp.dot(weights, taps, preferred_element_type=F32)
        total = acc_near[...] + part[128:192]
        acc_near[...] = acc_far[...] + part[64:128]
        acc_far[...] = part[0:64]

        @pl.when(q >= 2)
        def _():
            center = src[q - 1].astype(F32)
            emit(q - 2, (center + jnp.tanh(total + bias)).astype(BF16))

        return carry

    lax.fori_loop(0, count, body, 0)


def forecast_kernel(
    x_ref, kernel_ref, offset_ref, position_ref, slots_ref, reading_ref, precision_ref,
    part_ref,
    mats_ref, xin, wide, mid, acc_near, acc_far, rem, fields, weights_ref, flat, slab, code, code_mem, lanes,
    relay, own_pred, preds, sums,
    load_sem, halo_send, halo_recv, relay_send, relay_recv, start_send, start_recv,
    y_send, y_recv, c_send, c_recv, g_send, g_recv, code_sem,
    p_send, p_recv, z_send, z_recv, s_send, s_recv, h_send, h_recv,
):
    g = lax.axis_index("member")
    b = lax.axis_index("band")
    ypeer = {"member": g ^ 2}
    cpeer = {"member": g ^ 1}
    up = {"band": lax.rem(b + 1, 32)}
    down = {"band": lax.rem(b + 31, 32)}
    z = lax.rem(b, 4)
    xx = lax.rem(b // 4, 4)
    hi = b // 16
    members = [ypeer, cpeer, {"member": g ^ 3}]
    zs = [{"band": b - z + lax.rem(z + d, 4)} for d in (1, 2, 3)]
    xs = [{"band": hi * 16 + lax.rem(xx + d, 4) * 4 + z} for d in (1, 2, 3)]
    far = {"band": lax.rem(b + 16, 32), "member": g ^ 2}
    edge_low = b == 15
    edge_high = b == 16
    edge = jnp.logical_or(edge_low, edge_high)
    relaying = functools.reduce(jnp.logical_or, [b == band for band, _, _ in RELAYS])
    across = {"band": jnp.where(edge_low, 16, 15), "member": g ^ 2}

    barrier = pltpu.get_barrier_semaphore()
    for peer in members + zs + xs + [far, up, down]:
        pl.semaphore_signal(barrier, inc=1, device_id=peer)

    @pl.when(edge)
    def _():
        pl.semaphore_signal(barrier, inc=1, device_id=across)
        for band, _, k in RELAYS:
            pl.semaphore_signal(
                barrier, inc=1, device_id={"band": band, "member": g ^ 2 if k > 2 else g}
            )

    for band, _, k in RELAYS:
        @pl.when(b == band)
        def _():
            for target in (15, 16):
                pl.semaphore_signal(
                    barrier, inc=1, device_id={"band": target, "member": g ^ 2 if k > 2 else g}
                )

    def load(m):
        return pltpu.make_async_copy(x_ref.at[m], xin.at[m, 2:10], load_sem.at[m])

    for m in ORDER:
        load(m).start()
    pl.semaphore_wait(barrier, 12 + jnp.where(edge, 11, 0) + jnp.where(relaying, 2, 0))

    def halo_up(slot, src, peer=up):
        return remote(src, xin.at[slot, 0:2], halo_send.at[slot, 0], halo_recv.at[slot, 0], peer)

    def halo_down(slot, src, peer=down):
        return remote(src, xin.at[slot, 10:12], halo_send.at[slot, 1], halo_recv.at[slot, 1], peer)

    def to_relay(slot, src, side, k):
        band = next(band for band, s, n in RELAYS if (s, n) == (side, k))
        peer = {"band": band, "member": g ^ 2 if k > 2 else g}
        return remote(src, relay, halo_send.at[slot, side], relay_recv, peer)

    def edge_rows(n):
        m = ORDER[n]
        for r in range(2):
            k = 2 * n + r
            for side, is_edge, source, row, peer in (
                (0, edge_low, 6 + r, r, up), (1, edge_high, r, 10 + r, down),
            ):
                @pl.when(is_edge)
                def _():
                    src = x_ref.at[m, source : source + 1]
                    if k:
                        to_relay(m, src, side, k).start()
                    else:
                        remote(
                            src, xin.at[m, row : row + 1],
                            halo_send.at[m, side], halo_recv.at[m, side], peer,
                        ).start()

    not_low = jnp.logical_and(b < 31, jnp.logical_not(edge_low))
    not_high = jnp.logical_and(b > 0, jnp.logical_not(edge_high))

    def own_halo(n):
        m = ORDER[n]

        @pl.when(not_low)
        def _():
            halo_up(m, x_ref.at[m, 6:8]).start()

        @pl.when(not_high)
        def _():
            halo_down(m, x_ref.at[m, 0:2]).start()

        if n < 3:
            edge_rows(n)

    def start_copy():
        return remote(x_ref.at[0], xin.at[4, 2:10], start_send, start_recv, ypeer)

    own_halo(0)
    start_copy().start()
    for n in (1, 2, 3):
        own_halo(n)

    @pl.when(edge_low)
    def _():
        halo_up(4, x_ref.at[0, 6:8], across).start()

    @pl.when(edge_high)
    def _():
        halo_down(4, x_ref.at[0, 0:2], across).start()

    pos = position_ref[...]
    q5 = jnp.right_shift(pos, 5)
    flat_row = jnp.right_shift(q5 * 46604, 21)
    lon = pos - flat_row * LON
    row = jnp.right_shift(flat_row, 6)
    part = jnp.right_shift(row, 2)
    j = row - part * 4
    lane = jnp.where(lon < MAIN, j * MAIN + lon, 4 * MAIN + 32 * j + lon - MAIN)
    block = jnp.right_shift(lane, 7)
    code[...] = block * 128 + part * 64 + flat_row - row * 64
    lanes[...] = lane - block * 128
    to_scalar = pltpu.make_async_copy(code, code_mem, code_sem)
    to_scalar.start()

    for tap in range(3):
        weights_ref[64 * tap : 64 * tap + 64] = jnp.concatenate(
            [kernel_ref[tap, 0], kernel_ref[tap, 1], kernel_ref[tap, 2]], axis=1
        )
    square = (64, 64)
    diagonal = lax.broadcasted_iota(jnp.int32, square, 0) == lax.broadcasted_iota(jnp.int32, square, 1)
    bias = jnp.sum(
        jnp.where(diagonal, jnp.broadcast_to(offset_ref[...], square), 0.0), axis=1, keepdims=True
    )
    to_scalar.wait()

    def relay_copy(side, k):
        m = ORDER[k // 2]
        row = (0 if side == 0 else 10) + k % 2
        peer = {"band": 16 if side == 0 else 15, "member": g ^ 2 if k > 2 else g}
        return remote(relay, xin.at[m, row : row + 1], relay_send, halo_recv.at[m, side], peer)

    def relay_now(ks):
        for band, side, k in RELAYS:
            if k in ks:
                @pl.when(b == band)
                def _():
                    remote(x_ref.at[0, 0:1], relay, relay_send, relay_recv, up).wait_recv()
                    relay_copy(side, k).start()

    relay_now((1,))

    def piece(p, count):
        if count == 1:
            return (slice(None),) * 3
        if count == 4:
            return (p // 2, pl.ds(lax.rem(p, 2) * 32, 32), slice(None))
        return (p // 4, pl.ds(lax.rem(p, 4) * 16, 16), slice(None))

    def y_copy(m, p, count):
        at = piece(p, count)
        k = YBASE[m] + p
        return remote(
            fields.at[(0, m) + at], fields.at[(2, m) + at], y_send.at[k], y_recv.at[k], ypeer
        )

    def g_copy(m, p, count):
        at = piece(p, count)
        k = YBASE[m] + p
        return remote(
            fields.at[(2, m) + at], fields.at[(3, m) + at], g_send.at[k], g_recv.at[k], cpeer
        )

    def start_g():
        return remote(fields.at[2, 0], fields.at[3, 0], g_send.at[0], g_recv.at[0], cpeer)

    def c_copy(m):
        return remote(fields.at[0, m], fields.at[1, m], c_send.at[m], c_recv.at[m], cpeer)

    pred_copies = [
        remote(own_pred, preds.at[g], p_send.at[d], p_recv.at[d], members[d]) for d in range(3)
    ]

    def iteration(i, carry):
        slot = jnp.where(i == 4, 4, lax.rem(i + 1, 4))
        home = jnp.where(i == 4, 2, 0)
        own = lax.rem(slot, 4)

        @pl.when(i < 4)
        def _():
            load(slot).wait()

        @pl.when(b > 0)
        def _():
            halo_up(slot, x_ref.at[0, 6:8]).wait_recv()

        @pl.when(b < 31)
        def _():
            halo_down(slot, x_ref.at[0, 0:2]).wait_recv()

        @pl.when(b == 0)
        def _():
            xin[slot, 0:2] = jnp.zeros((2, 64, LON), BF16)

        @pl.when(b == 31)
        def _():
            xin[slot, 10:12] = jnp.zeros((2, 64, LON), BF16)

        def spread(r, c):
            wide[r] = widen(xin[slot, r])
            return c

        lax.fori_loop(0, 12, spread, 0)
        weights = weights_ref[...]

        def emit_mid(r, value):
            mid[r] = value

        conv_rows(wide, 12, weights, bias, acc_near, acc_far, emit_mid)

        @pl.when(b == 0)
        def _():
            mid[0] = jnp.zeros((64, WIDE), BF16)

        @pl.when(b == 31)
        def _():
            mid[9] = jnp.zeros((64, WIDE), BF16)

        def emit_field(r, value):
            half = r // 4
            offset = pl.multiple_of(lax.rem(r, 4) * MAIN, 128)
            fields[home, own, half, :, pl.ds(offset, MAIN)] = value[:, :MAIN]
            rem[r] = value[:, MAIN:WIDE]

        conv_rows(mid, 10, weights, bias, acc_near, acc_far, emit_field)
        lane = lax.broadcasted_iota(jnp.int32, (64, 128), 1)
        for half in range(2):
            tail = rem[4 * half]
            for j in range(1, 4):
                tail = jnp.where(lane < 32 * j, tail, pltpu.roll(rem[4 * half + j], 32 * j, 1))
            fields[home, own, half, :, 4 * MAIN : PACK] = tail

        @pl.when(i < 4)
        def _():
            c_copy(slot).start()

        @pl.when(i == 0)
        def _():
            y_copy(1, 0, 1).start()

            relay_now((2, 3))

        @pl.when(i == 1)
        def _():
            for p in range(3):
                y_copy(2, p, 4).start()
            relay_now((4, 5))
            start_copy().wait_recv()

            @pl.when(not_low)
            def _():
                halo_up(4, xin.at[4, 8:10]).start()

            @pl.when(not_high)
            def _():
                halo_down(4, xin.at[4, 2:4]).start()

            @pl.when(edge_low)
            def _():
                halo_up(0, xin.at[4, 8:10], across).start()

            @pl.when(edge_high)
            def _():
                halo_down(0, xin.at[4, 2:4], across).start()

        @pl.when(i < 4)
        def _():
            for half in range(2):
                widen_field(fields.at[0, slot, half], flat.at[slot], half)

        @pl.when(i == 3)
        def _():
            pick_loop(code_mem, lanes, own_pred, flat, slab)
            for c in pred_copies:
                c.start()
            y_copy(2, 3, 4).start()
            for p in range(8):
                y_copy(3, p, 8).start()
            y_copy(1, 0, 1).wait_recv()
            g_copy(1, 0, 1).start()

        @pl.when(i == 4)
        def _():
            start_g().start()

        return carry

    lax.fori_loop(0, 5, iteration, 0)

    for c in pred_copies:
        c.wait()
    preds[g] = own_pred[...]
    predicted = jnp.concatenate([preds[d, 0:4] for d in range(4)], axis=0)

    def line(ref):
        return jnp.concatenate([ref[n : n + 1] for n in range(16)], axis=1)

    live = (lax.broadcasted_iota(jnp.int32, (1, 2048), 1) < slots_ref[0]).astype(F32)
    mean = jnp.sum(predicted, axis=0, keepdims=True) * (1.0 / 16.0)
    anomaly = predicted - mean
    weighted = anomaly * (line(precision_ref) * live)
    gram = exact(weighted, anomaly, (((1,), (1,)), ((), ())))
    drive = jnp.sum(weighted * (line(reading_ref) - mean), axis=1, keepdims=True)
    pair = jnp.concatenate([gram, drive, jnp.zeros((16, 111), F32)], axis=1)

    def reduce(stage, place, pair, peers, sends, recvs):
        sums[stage, place] = pair
        copies = [
            remote(sums.at[stage, place], sums.at[stage, place], sends.at[d], recvs.at[d], peer)
            for d, peer in enumerate(peers)
        ]
        for c in copies:
            c.start()
        for c in copies:
            c.wait()

    reduce(0, z, pair, zs, z_send, z_recv)
    pair = (sums[0, 0] + sums[0, 1]) + (sums[0, 2] + sums[0, 3])
    reduce(1, xx, pair, xs, s_send, s_recv)
    pair = (sums[1, 0] + sums[1, 1]) + (sums[1, 2] + sums[1, 3])
    reduce(2, hi, pair, [far], h_send, h_recv)
    pair = sums[2, 0] + sums[2, 1]
    mixing = transform(pair[:, 0:16], pair[:, 16:17]).astype(BF16)
    mats_ref[...] = expand(mixing, g)

    mats = mats_ref[...]

    def mix(p):
        half = p // 4
        rows = pl.ds(pl.multiple_of(lax.rem(p, 4) * 16, 16), 16)

        def product(lo, width):
            block = fields[:, :, half, rows, lo : lo + width].reshape(256, width)
            out = jnp.dot(mats, block, preferred_element_type=F32)
            return out.astype(BF16).reshape(4, 16, width)

        tail = product(4 * MAIN, 128)
        for j in range(4):
            part_ref[:, 4 * half + j, rows, 0:MAIN] = product(j * MAIN, MAIN)
            part_ref[:, 4 * half + j, rows, MAIN:LON] = tail[:, :, 32 * j : 32 * j + 32]

    def forward(m, count):
        def body(p, carry):
            y_copy(m, p, count).wait_recv()
            g_copy(m, p, count).start()
            return carry

        lax.fori_loop(0, count, body, 0)

    forward(2, 4)
    g_copy(1, 0, 1).wait_recv()
    start_g().wait_recv()
    for m in range(4):
        c_copy(m).wait_recv()

    def early(p, carry):
        g_copy(2, p, 4).wait_recv()
        return carry

    lax.fori_loop(0, 4, early, 0)
    def blend(p, carry):
        y_copy(3, p, 8).wait_recv()
        g_copy(3, p, 8).start()

        @pl.when(p > 0)
        def _():
            g_copy(3, p - 1, 8).wait_recv()
            mix(p - 1)

        return carry

    lax.fori_loop(0, 8, blend, 0)
    g_copy(3, 7, 8).wait_recv()
    mix(7)
    start_copy().wait_send()
    for slot in range(5):
        @pl.when(b < 31)
        def _():
            halo_up(slot, x_ref.at[0, 6:8]).wait_send()

        @pl.when(b > 0)
        def _():
            halo_down(slot, x_ref.at[0, 0:2]).wait_send()

    @pl.when(relaying)
    def _():
        relay_copy(0, 1).wait_send()

    start_g().wait_send()
    for m, count in ((1, 1), (2, 4), (3, 8)):
        def finish(p, carry):
            y_copy(m, p, count).wait_send()
            g_copy(m, p, count).wait_send()
            return carry

        lax.fori_loop(0, count, finish, 0)
    for m in range(4):
        c_copy(m).wait_send()


def run_forecast(x, kernel, offset, position, slots, reading, precision):
    dma = pltpu.SemaphoreType.DMA
    return pl.pallas_call(
        forecast_kernel,
        out_shape=pltpu.VMEM((4, 8, 64, LON), BF16),
        in_specs=[ANY, VM, VM, VM, SM, VM, VM],
        out_specs=VM,
        scratch_shapes=[
            pltpu.VMEM((64, 256), BF16),
            pltpu.VMEM((5, 12, 64, LON), BF16),
            pltpu.VMEM((12, 64, WIDE), BF16),
            pltpu.VMEM((10, 64, WIDE), BF16),
            pltpu.VMEM((64, WIDE), F32),
            pltpu.VMEM((64, WIDE), F32),
            pltpu.VMEM((8, 64, 128), BF16),
            pltpu.VMEM((4, 4, 2, 64, PACK), BF16),
            pltpu.VMEM((192, 192), BF16),
            pltpu.VMEM((4, PACK, 128), F32),
            pltpu.VMEM((4, 128, 128), F32),
            pltpu.VMEM((16, 128), jnp.int32),
            pltpu.SMEM((16, 128), jnp.int32),
            pltpu.VMEM((16, 128), jnp.int32),
            pltpu.VMEM((1, 64, LON), BF16),
            pltpu.VMEM((8, 2048), F32),
            pltpu.VMEM((4, 8, 2048), F32),
            pltpu.VMEM((3, 4, 16, 128), F32),
            dma((4,)), dma((5, 2)), dma((5, 2)), dma, dma, dma, dma,
            dma((14,)), dma((14,)), dma((4,)), dma((4,)), dma((14,)), dma((14,)), dma,
            dma((3,)), dma((3,)), dma((3,)), dma((3,)), dma((3,)), dma((3,)), dma((1,)), dma((1,)),
        ],
        compiler_params=pltpu.CompilerParams(
            collective_id=1, has_side_effects=True, vmem_limit_bytes=53 << 20
        ),
        name="forecast",
    )(x, kernel, offset, position, slots, reading, precision)


def widen_field(src, dst, half):
    for block in range(45):
        start = block * 128
        dst[start + half * 64 : start + half * 64 + 64, :] = src[:, start : start + 128].astype(F32)


def pick_loop(code_mem, lanes, p_ref, flat, slab):
    square = (128, 128)
    down = lax.broadcasted_iota(jnp.int32, square, 0)
    diagonal = down == lax.broadcasted_iota(jnp.int32, square, 1)

    def group(n, carry):
        def fetch(t, c):
            for u in range(8):
                slot = t * 8 + u
                place = code_mem[n, slot]
                for m in range(4):
                    slab[m, pl.ds(slot, 1), :] = flat[m, pl.ds(place, 1), :]
            return c

        lax.fori_loop(0, 16, fetch, 0)
        hot = jnp.where(down == lanes[pl.ds(n, 1), :], 1.0, 0.0).astype(BF16)
        picked = []
        for m in range(4):
            table = jnp.dot(slab[m].astype(BF16), hot, preferred_element_type=F32)
            picked.append(jnp.sum(jnp.where(diagonal, table, 0.0), axis=0, keepdims=True))
        picked.append(jnp.zeros((4, 128), F32))
        p_ref[:, pl.ds(pl.multiple_of(n * 128, 128), 128)] = jnp.concatenate(picked, axis=0)
        return carry

    lax.fori_loop(0, 16, group, 0)


def exact(a, b, dims=(((1,), (0,)), ((), ()))):
    return lax.dot_general(
        a, b, dims, precision=lax.Precision.HIGHEST, preferred_element_type=F32
    )


def transform(gram, drive):
    n = 16
    eye = (
        lax.broadcasted_iota(jnp.int32, (n, n), 0) == lax.broadcasted_iota(jnp.int32, (n, n), 1)
    ).astype(F32)
    system = eye + gram / (n - 1.0)
    scale = jnp.sum(jnp.sum(system * eye, axis=1, keepdims=True), axis=0, keepdims=True)
    iterate = system / scale
    root = eye
    for _ in range(NS_STEPS):
        factor = 0.5 * (3.0 * eye - exact(root, iterate))
        iterate = exact(iterate, factor)
        root = exact(factor, root)
    spread = root / jnp.sqrt(scale)
    mean_weights = exact(exact(root, root), drive) / (scale * (n - 1.0))
    centering = eye - 1.0 / n
    return 1.0 / n + exact(centering, mean_weights + spread)


def expand(mixing, g):
    def iota(shape, dim):
        return lax.broadcasted_iota(jnp.int32, shape, dim)

    own = (iota((64, 16), 1) == 4 * g + iota((64, 16), 0) // 16).astype(BF16)
    column = iota((16, 256), 1)
    source = 4 * jnp.bitwise_xor(column // 64, g) + lax.rem(column // 16, 4)
    order = (iota((16, 256), 0) == source).astype(BF16)
    picked = lax.dot_general(
        own, mixing, (((1,), (1,)), ((), ())), preferred_element_type=F32
    ).astype(BF16)
    full = jnp.dot(picked, order, preferred_element_type=F32)
    same = lax.rem(iota((64, 256), 0), 16) == lax.rem(iota((64, 256), 1), 16)
    return jnp.where(same, full, 0.0).astype(BF16)


def finish_kernel(part_ref, o_ref, sem):
    copies = [
        pltpu.make_async_copy(
            part_ref.at[n // 2, pl.ds(n % 2 * 4, 4)], o_ref.at[n // 2, pl.ds(n % 2 * 4, 4)], sem.at[n]
        )
        for n in range(8)
    ]
    for copy in copies:
        copy.start()
    for copy in copies:
        copy.wait()


def run_finish(part):
    return pl.pallas_call(
        finish_kernel,
        out_shape=jax.ShapeDtypeStruct((4, 8, 64, LON), BF16),
        in_specs=[VM],
        out_specs=ANY,
        scratch_shapes=[pltpu.SemaphoreType.DMA((8,))],
        compiler_params=pltpu.CompilerParams(vmem_limit_bytes=1 << 20),
        name="finish",
    )(part)


def local(x, kernel, offset, position, slots, reading, precision):
    part = run_forecast(
        x,
        kernel,
        offset.reshape(1, 64),
        position.reshape(16, 128),
        slots,
        reading.reshape(16, 128),
        precision.reshape(16, 128),
    )
    return run_finish(part)


def solution(mesh):
    return jax.shard_map(
        local,
        mesh=mesh,
        in_specs=(
            P("member", "band", None, None), P(), P(), P("band"), P("band"), P("band"), P("band"),
        ),
        out_specs=P("member", "band", None, None),
        check_vma=False,
    )
```

```python
import functools

import jax
import jax.numpy as jnp
from jax import lax
from jax.experimental import pallas as pl
from jax.experimental.pallas import tpu as pltpu
from jax.sharding import PartitionSpec as P

NS_STEPS = 16
LON = 1440
WIDE = 1536
MAIN = 1408
PACK = 5760
F32 = jnp.float32
BF16 = jnp.bfloat16
ORDER = (1, 2, 3, 0)
YBASE = {1: 1, 2: 2, 3: 6}
RELAYS = (
    (23, 0, 1), (27, 0, 2), (21, 0, 3), (22, 0, 4), (31, 0, 5),
    (8, 1, 1), (4, 1, 2), (10, 1, 3), (9, 1, 4), (0, 1, 5),
)
ANY = pl.BlockSpec(memory_space=pl.ANY)
VM = pl.BlockSpec(memory_space=pltpu.VMEM)
SM = pl.BlockSpec(memory_space=pltpu.SMEM)


def remote(src, dst, send, recv, peer):
    return pltpu.make_async_remote_copy(
        src_ref=src, dst_ref=dst, send_sem=send, recv_sem=recv, device_id=peer
    )


def widen(x):
    last = jnp.concatenate(
        [x[:, MAIN:LON], x[:, 0:32], x[:, 0:32], x[:, MAIN:LON]], axis=1
    )
    return jnp.concatenate([x[:, :MAIN], last], axis=1)


def conv_rows(src, count, weights, bias, acc_near, acc_far, emit):
    def body(q, carry):
        row = src[q]
        taps = jnp.concatenate(
            [pltpu.roll(row, 1, 1), row, pltpu.roll(row, WIDE - 1, 1)], axis=0
        )
        part = jnp.dot(weights, taps, preferred_element_type=F32)
        total = acc_near[...] + part[128:192]
        acc_near[...] = acc_far[...] + part[64:128]
        acc_far[...] = part[0:64]

        @pl.when(q >= 2)
        def _():
            center = src[q - 1].astype(F32)
            emit(q - 2, (center + jnp.tanh(total + bias)).astype(BF16))

        return carry

    lax.fori_loop(0, count, body, 0)


def forecast_kernel(
    x_ref, kernel_ref, offset_ref, position_ref, slots_ref, reading_ref, precision_ref,
    part_ref,
    mats_ref, xin, wide, mid, acc_near, acc_far, rem, fields, weights_ref, flat, slab, code, code_mem, lanes,
    relay, own_pred, dense, tail_out, tail_in, preds, sums,
    load_sem, halo_send, halo_recv, relay_send, relay_recv, start_send, start_recv,
    y_send, y_recv, c_send, c_recv, g_send, g_recv, code_sem,
    p_send, p_recv, z_send, z_recv, s_send, s_recv, h_send, h_recv,
):
    g = lax.axis_index("member")
    b = lax.axis_index("band")
    ypeer = {"member": g ^ 2}
    cpeer = {"member": g ^ 1}
    up = {"band": lax.rem(b + 1, 32)}
    down = {"band": lax.rem(b + 31, 32)}
    z = lax.rem(b, 4)
    xx = lax.rem(b // 4, 4)
    hi = b // 16
    members = [ypeer, cpeer, {"member": g ^ 3}]
    zs = [{"band": b - z + lax.rem(z + d, 4)} for d in (1, 2, 3)]
    xs = [{"band": hi * 16 + lax.rem(xx + d, 4) * 4 + z} for d in (1, 2, 3)]
    far = {"band": lax.rem(b + 16, 32), "member": g ^ 2}
    edge_low = b == 15
    edge_high = b == 16
    edge = jnp.logical_or(edge_low, edge_high)
    relaying = functools.reduce(jnp.logical_or, [b == band for band, _, _ in RELAYS])
    across = {"band": jnp.where(edge_low, 16, 15), "member": g ^ 2}

    barrier = pltpu.get_barrier_semaphore()
    for peer in members + zs + xs + [far, up, down]:
        pl.semaphore_signal(barrier, inc=1, device_id=peer)

    @pl.when(edge)
    def _():
        pl.semaphore_signal(barrier, inc=1, device_id=across)
        for band, _, k in RELAYS:
            pl.semaphore_signal(
                barrier, inc=1, device_id={"band": band, "member": g ^ 2 if k > 2 else g}
            )

    for band, _, k in RELAYS:
        @pl.when(b == band)
        def _():
            for target in (15, 16):
                pl.semaphore_signal(
                    barrier, inc=1, device_id={"band": target, "member": g ^ 2 if k > 2 else g}
                )

    def load(m):
        return pltpu.make_async_copy(x_ref.at[m], xin.at[m, 2:10], load_sem.at[m])

    for m in (0, 1, 2, 3):
        load(m).start()
    pl.semaphore_wait(barrier, 12 + jnp.where(edge, 11, 0) + jnp.where(relaying, 2, 0))

    def halo_up(slot, src, peer=up):
        return remote(src, xin.at[slot, 0:2], halo_send.at[slot, 0], halo_recv.at[slot, 0], peer)

    def halo_down(slot, src, peer=down):
        return remote(src, xin.at[slot, 10:12], halo_send.at[slot, 1], halo_recv.at[slot, 1], peer)

    def to_relay(slot, src, side, k):
        band = next(band for band, s, n in RELAYS if (s, n) == (side, k))
        peer = {"band": band, "member": g ^ 2 if k > 2 else g}
        return remote(src, relay, halo_send.at[slot, side], relay_recv, peer)

    def edge_rows(n):
        m = ORDER[n]
        for r in range(2):
            k = 2 * n + r
            for side, is_edge, source, row, peer in (
                (0, edge_low, 6 + r, r, up), (1, edge_high, r, 10 + r, down),
            ):
                @pl.when(is_edge)
                def _():
                    src = x_ref.at[m, source : source + 1]
                    if k:
                        to_relay(m, src, side, k).start()
                    else:
                        remote(
                            src, xin.at[m, row : row + 1],
                            halo_send.at[m, side], halo_recv.at[m, side], peer,
                        ).start()

    not_low = jnp.logical_and(b < 31, jnp.logical_not(edge_low))
    not_high = jnp.logical_and(b > 0, jnp.logical_not(edge_high))

    def own_halo(n):
        m = ORDER[n]

        @pl.when(not_low)
        def _():
            halo_up(m, x_ref.at[m, 6:8]).start()

        @pl.when(not_high)
        def _():
            halo_down(m, x_ref.at[m, 0:2]).start()

        if n < 3:
            edge_rows(n)

    def start_copy():
        return remote(
            x_ref.at[0, :, :, 0:MAIN], xin.at[4, 2:10, :, 0:MAIN],
            start_send.at[0], start_recv.at[0], ypeer,
        )

    def tail_copy():
        return remote(tail_out, tail_in, start_send.at[1], start_recv.at[1], ypeer)

    own_halo(0)
    start_copy().start()
    for n in (1, 2, 3):
        own_halo(n)

    @pl.when(edge_low)
    def _():
        halo_up(4, x_ref.at[0, 6:8], across).start()

    @pl.when(edge_high)
    def _():
        halo_down(4, x_ref.at[0, 0:2], across).start()

    load(0).wait()
    for half in range(2):
        tail_out[half] = jnp.concatenate(
            [xin[0, 2 + 4 * half + j, :, MAIN:LON] for j in range(4)], axis=1
        )
    tail_copy().start()

    pos = position_ref[...]
    q5 = jnp.right_shift(pos, 5)
    flat_row = jnp.right_shift(q5 * 46604, 21)
    lon = pos - flat_row * LON
    row = jnp.right_shift(flat_row, 6)
    part = jnp.right_shift(row, 2)
    j = row - part * 4
    lane = jnp.where(lon < MAIN, j * MAIN + lon, 4 * MAIN + 32 * j + lon - MAIN)
    block = jnp.right_shift(lane, 7)
    code[...] = block * 128 + part * 64 + flat_row - row * 64
    lanes[...] = lane - block * 128
    to_scalar = pltpu.make_async_copy(code, code_mem, code_sem)
    to_scalar.start()

    for tap in range(3):
        weights_ref[64 * tap : 64 * tap + 64] = jnp.concatenate(
            [kernel_ref[tap, 0], kernel_ref[tap, 1], kernel_ref[tap, 2]], axis=1
        )
    square = (64, 64)
    diagonal = lax.broadcasted_iota(jnp.int32, square, 0) == lax.broadcasted_iota(jnp.int32, square, 1)
    bias = jnp.sum(
        jnp.where(diagonal, jnp.broadcast_to(offset_ref[...], square), 0.0), axis=1, keepdims=True
    )
    to_scalar.wait()

    def relay_copy(side, k):
        m = ORDER[k // 2]
        row = (0 if side == 0 else 10) + k % 2
        peer = {"band": 16 if side == 0 else 15, "member": g ^ 2 if k > 2 else g}
        return remote(relay, xin.at[m, row : row + 1], relay_send, halo_recv.at[m, side], peer)

    def relay_now(ks):
        for band, side, k in RELAYS:
            if k in ks:
                @pl.when(b == band)
                def _():
                    remote(x_ref.at[0, 0:1], relay, relay_send, relay_recv, up).wait_recv()
                    relay_copy(side, k).start()

    relay_now((1,))

    def piece(p, count):
        if count == 1:
            return (slice(None),) * 3
        if count == 4:
            return (p // 2, pl.ds(lax.rem(p, 2) * 32, 32), slice(None))
        return (p // 4, pl.ds(lax.rem(p, 4) * 16, 16), slice(None))

    def y_copy(m, p, count):
        at = piece(p, count)
        k = YBASE[m] + p
        return remote(
            fields.at[(0, m) + at], fields.at[(2, m) + at], y_send.at[k], y_recv.at[k], ypeer
        )

    def g_copy(m, p, count):
        at = piece(p, count)
        k = YBASE[m] + p
        return remote(
            fields.at[(2, m) + at], fields.at[(3, m) + at], g_send.at[k], g_recv.at[k], cpeer
        )

    def start_g():
        return remote(fields.at[2, 0], fields.at[3, 0], g_send.at[0], g_recv.at[0], cpeer)

    def c_copy(m):
        return remote(fields.at[0, m], fields.at[1, m], c_send.at[m], c_recv.at[m], cpeer)

    pred_copies = [
        remote(dense, preds.at[g], p_send.at[d], p_recv.at[d], members[d]) for d in range(3)
    ]

    def iteration(i, carry):
        slot = jnp.where(i == 4, 4, lax.rem(i + 1, 4))
        home = jnp.where(i == 4, 2, 0)
        own = lax.rem(slot, 4)

        @pl.when(i < 3)
        def _():
            load(slot).wait()

        @pl.when(b > 0)
        def _():
            halo_up(slot, x_ref.at[0, 6:8]).wait_recv()

        @pl.when(b < 31)
        def _():
            halo_down(slot, x_ref.at[0, 0:2]).wait_recv()

        @pl.when(b == 0)
        def _():
            xin[slot, 0:2] = jnp.zeros((2, 64, LON), BF16)

        @pl.when(b == 31)
        def _():
            xin[slot, 10:12] = jnp.zeros((2, 64, LON), BF16)

        def spread(r, c):
            wide[r] = widen(xin[slot, r])
            return c

        lax.fori_loop(0, 12, spread, 0)
        weights = weights_ref[...]

        def emit_mid(r, value):
            mid[r] = value

        conv_rows(wide, 12, weights, bias, acc_near, acc_far, emit_mid)

        @pl.when(b == 0)
        def _():
            mid[0] = jnp.zeros((64, WIDE), BF16)

        @pl.when(b == 31)
        def _():
            mid[9] = jnp.zeros((64, WIDE), BF16)

        def emit_field(r, value):
            half = r // 4
            offset = pl.multiple_of(lax.rem(r, 4) * MAIN, 128)
            fields[home, own, half, :, pl.ds(offset, MAIN)] = value[:, :MAIN]
            rem[r] = value[:, MAIN:WIDE]

        conv_rows(mid, 10, weights, bias, acc_near, acc_far, emit_field)
        lane = lax.broadcasted_iota(jnp.int32, (64, 128), 1)
        for half in range(2):
            tail = rem[4 * half]
            for j in range(1, 4):
                tail = jnp.where(lane < 32 * j, tail, pltpu.roll(rem[4 * half + j], 32 * j, 1))
            fields[home, own, half, :, 4 * MAIN : PACK] = tail

        @pl.when(i < 4)
        def _():
            c_copy(slot).start()

        @pl.when(i == 0)
        def _():
            y_copy(1, 0, 1).start()

            relay_now((2, 3))

        @pl.when(i == 1)
        def _():
            for p in range(3):
                y_copy(2, p, 4).start()
            relay_now((4, 5))
            start_copy().wait_recv()
            tail_copy().wait_recv()
            for half in range(2):
                for j in range(4):
                    xin[4, 2 + 4 * half + j, :, MAIN:LON] = tail_in[half, :, 32 * j : 32 * j + 32]

            @pl.when(not_low)
            def _():
                halo_up(4, xin.at[4, 8:10]).start()

            @pl.when(not_high)
            def _():
                halo_down(4, xin.at[4, 2:4]).start()

            @pl.when(edge_low)
            def _():
                halo_up(0, xin.at[4, 8:10], across).start()

            @pl.when(edge_high)
            def _():
                halo_down(0, xin.at[4, 2:4], across).start()

        @pl.when(i < 4)
        def _():
            for half in range(2):
                widen_field(fields.at[0, slot, half], flat.at[slot], half)

        @pl.when(i == 3)
        def _():
            pick_loop(code_mem, lanes, own_pred, flat, slab)
            dense[...] = jnp.concatenate(
                [own_pred[m : m + 1, 512 * q : 512 * q + 512] for m in range(4) for q in range(4)],
                axis=0,
            ).astype(BF16)
            for c in pred_copies:
                c.start()
            y_copy(2, 3, 4).start()
            for p in range(8):
                y_copy(3, p, 8).start()
            y_copy(1, 0, 1).wait_recv()
            g_copy(1, 0, 1).start()

        @pl.when(i == 4)
        def _():
            start_g().start()

        return carry

    lax.fori_loop(0, 5, iteration, 0)

    for c in pred_copies:
        c.wait()
    preds[g] = dense[...]
    quarters = preds[...].astype(F32)
    predicted = jnp.concatenate(
        [
            jnp.concatenate([quarters[d, 4 * m + q : 4 * m + q + 1] for q in range(4)], axis=1)
            for d in range(4)
            for m in range(4)
        ],
        axis=0,
    )

    def line(ref):
        return jnp.concatenate([ref[n : n + 1] for n in range(16)], axis=1)

    live = (lax.broadcasted_iota(jnp.int32, (1, 2048), 1) < slots_ref[0]).astype(F32)
    mean = jnp.sum(predicted, axis=0, keepdims=True) * (1.0 / 16.0)
    anomaly = predicted - mean
    weighted = anomaly * (line(precision_ref) * live)
    gram = exact(weighted, anomaly, (((1,), (1,)), ((), ())))
    drive = jnp.sum(weighted * (line(reading_ref) - mean), axis=1, keepdims=True)
    pair = jnp.concatenate([gram, drive, jnp.zeros((16, 111), F32)], axis=1)

    def reduce(stage, place, pair, peers, sends, recvs):
        sums[stage, place] = pair
        copies = [
            remote(sums.at[stage, place], sums.at[stage, place], sends.at[d], recvs.at[d], peer)
            for d, peer in enumerate(peers)
        ]
        for c in copies:
            c.start()
        for c in copies:
            c.wait()

    reduce(0, z, pair, zs, z_send, z_recv)
    pair = (sums[0, 0] + sums[0, 1]) + (sums[0, 2] + sums[0, 3])
    reduce(1, xx, pair, xs, s_send, s_recv)
    pair = (sums[1, 0] + sums[1, 1]) + (sums[1, 2] + sums[1, 3])
    reduce(2, hi, pair, [far], h_send, h_recv)
    pair = sums[2, 0] + sums[2, 1]
    mixing = transform(pair[:, 0:16], pair[:, 16:17]).astype(BF16)
    mats_ref[...] = expand(mixing, g)

    mats = mats_ref[...]

    def mix(p):
        half = p // 4
        rows = pl.ds(pl.multiple_of(lax.rem(p, 4) * 16, 16), 16)

        def product(lo, width):
            block = fields[:, :, half, rows, lo : lo + width].reshape(256, width)
            out = jnp.dot(mats, block, preferred_element_type=F32)
            return out.astype(BF16).reshape(4, 16, width)

        tail = product(4 * MAIN, 128)
        for j in range(4):
            part_ref[:, 4 * half + j, rows, 0:MAIN] = product(j * MAIN, MAIN)
            part_ref[:, 4 * half + j, rows, MAIN:LON] = tail[:, :, 32 * j : 32 * j + 32]

    def forward(m, count):
        def body(p, carry):
            y_copy(m, p, count).wait_recv()
            g_copy(m, p, count).start()
            return carry

        lax.fori_loop(0, count, body, 0)

    forward(2, 4)
    g_copy(1, 0, 1).wait_recv()
    start_g().wait_recv()
    for m in range(4):
        c_copy(m).wait_recv()

    def early(p, carry):
        g_copy(2, p, 4).wait_recv()
        return carry

    lax.fori_loop(0, 4, early, 0)
    def blend(p, carry):
        y_copy(3, p, 8).wait_recv()
        g_copy(3, p, 8).start()

        @pl.when(p > 0)
        def _():
            g_copy(3, p - 1, 8).wait_recv()
            mix(p - 1)

        return carry

    lax.fori_loop(0, 8, blend, 0)
    g_copy(3, 7, 8).wait_recv()
    mix(7)
    start_copy().wait_send()
    tail_copy().wait_send()
    for slot in range(5):
        @pl.when(b < 31)
        def _():
            halo_up(slot, x_ref.at[0, 6:8]).wait_send()

        @pl.when(b > 0)
        def _():
            halo_down(slot, x_ref.at[0, 0:2]).wait_send()

    @pl.when(relaying)
    def _():
        relay_copy(0, 1).wait_send()

    start_g().wait_send()
    for m, count in ((1, 1), (2, 4), (3, 8)):
        def finish(p, carry):
            y_copy(m, p, count).wait_send()
            g_copy(m, p, count).wait_send()
            return carry

        lax.fori_loop(0, count, finish, 0)
    for m in range(4):
        c_copy(m).wait_send()


def run_forecast(x, kernel, offset, position, slots, reading, precision):
    dma = pltpu.SemaphoreType.DMA
    return pl.pallas_call(
        forecast_kernel,
        out_shape=pltpu.VMEM((4, 8, 64, LON), BF16),
        in_specs=[ANY, VM, VM, VM, SM, VM, VM],
        out_specs=VM,
        scratch_shapes=[
            pltpu.VMEM((64, 256), BF16),
            pltpu.VMEM((5, 12, 64, LON), BF16),
            pltpu.VMEM((12, 64, WIDE), BF16),
            pltpu.VMEM((10, 64, WIDE), BF16),
            pltpu.VMEM((64, WIDE), F32),
            pltpu.VMEM((64, WIDE), F32),
            pltpu.VMEM((8, 64, 128), BF16),
            pltpu.VMEM((4, 4, 2, 64, PACK), BF16),
            pltpu.VMEM((192, 192), BF16),
            pltpu.VMEM((4, PACK, 128), F32),
            pltpu.VMEM((4, 128, 128), F32),
            pltpu.VMEM((16, 128), jnp.int32),
            pltpu.SMEM((16, 128), jnp.int32),
            pltpu.VMEM((16, 128), jnp.int32),
            pltpu.VMEM((1, 64, LON), BF16),
            pltpu.VMEM((8, 2048), F32),
            pltpu.VMEM((16, 512), BF16),
            pltpu.VMEM((2, 64, 128), BF16),
            pltpu.VMEM((2, 64, 128), BF16),
            pltpu.VMEM((4, 16, 512), BF16),
            pltpu.VMEM((3, 4, 16, 128), F32),
            dma((4,)), dma((5, 2)), dma((5, 2)), dma, dma, dma((2,)), dma((2,)),
            dma((14,)), dma((14,)), dma((4,)), dma((4,)), dma((14,)), dma((14,)), dma,
            dma((3,)), dma((3,)), dma((3,)), dma((3,)), dma((3,)), dma((3,)), dma((1,)), dma((1,)),
        ],
        compiler_params=pltpu.CompilerParams(
            collective_id=1, has_side_effects=True, vmem_limit_bytes=53 << 20
        ),
        name="forecast",
    )(x, kernel, offset, position, slots, reading, precision)


def widen_field(src, dst, half):
    for block in range(45):
        start = block * 128
        dst[start + half * 64 : start + half * 64 + 64, :] = src[:, start : start + 128].astype(F32)


def pick_loop(code_mem, lanes, p_ref, flat, slab):
    square = (128, 128)
    down = lax.broadcasted_iota(jnp.int32, square, 0)
    diagonal = down == lax.broadcasted_iota(jnp.int32, square, 1)

    def group(n, carry):
        def fetch(t, c):
            for u in range(8):
                slot = t * 8 + u
                place = code_mem[n, slot]
                for m in range(4):
                    slab[m, pl.ds(slot, 1), :] = flat[m, pl.ds(place, 1), :]
            return c

        lax.fori_loop(0, 16, fetch, 0)
        hot = jnp.where(down == lanes[pl.ds(n, 1), :], 1.0, 0.0).astype(BF16)
        picked = []
        for m in range(4):
            table = jnp.dot(slab[m].astype(BF16), hot, preferred_element_type=F32)
            picked.append(jnp.sum(jnp.where(diagonal, table, 0.0), axis=0, keepdims=True))
        picked.append(jnp.zeros((4, 128), F32))
        p_ref[:, pl.ds(pl.multiple_of(n * 128, 128), 128)] = jnp.concatenate(picked, axis=0)
        return carry

    lax.fori_loop(0, 16, group, 0)


def exact(a, b, dims=(((1,), (0,)), ((), ()))):
    return lax.dot_general(
        a, b, dims, precision=lax.Precision.HIGHEST, preferred_element_type=F32
    )


def transform(gram, drive):
    n = 16
    eye = (
        lax.broadcasted_iota(jnp.int32, (n, n), 0) == lax.broadcasted_iota(jnp.int32, (n, n), 1)
    ).astype(F32)
    system = eye + gram / (n - 1.0)
    scale = jnp.sum(jnp.sum(system * eye, axis=1, keepdims=True), axis=0, keepdims=True)
    iterate = system / scale
    root = eye
    for _ in range(NS_STEPS):
        factor = 0.5 * (3.0 * eye - exact(root, iterate))
        iterate = exact(iterate, factor)
        root = exact(factor, root)
    spread = root / jnp.sqrt(scale)
    mean_weights = exact(exact(root, root), drive) / (scale * (n - 1.0))
    centering = eye - 1.0 / n
    return 1.0 / n + exact(centering, mean_weights + spread)


def expand(mixing, g):
    def iota(shape, dim):
        return lax.broadcasted_iota(jnp.int32, shape, dim)

    own = (iota((64, 16), 1) == 4 * g + iota((64, 16), 0) // 16).astype(BF16)
    column = iota((16, 256), 1)
    source = 4 * jnp.bitwise_xor(column // 64, g) + lax.rem(column // 16, 4)
    order = (iota((16, 256), 0) == source).astype(BF16)
    picked = lax.dot_general(
        own, mixing, (((1,), (1,)), ((), ())), preferred_element_type=F32
    ).astype(BF16)
    full = jnp.dot(picked, order, preferred_element_type=F32)
    same = lax.rem(iota((64, 256), 0), 16) == lax.rem(iota((64, 256), 1), 16)
    return jnp.where(same, full, 0.0).astype(BF16)


def finish_kernel(part_ref, o_ref, sem):
    copies = [
        pltpu.make_async_copy(
            part_ref.at[n // 2, pl.ds(n % 2 * 4, 4)], o_ref.at[n // 2, pl.ds(n % 2 * 4, 4)], sem.at[n]
        )
        for n in range(8)
    ]
    for copy in copies:
        copy.start()
    for copy in copies:
        copy.wait()


def run_finish(part):
    return pl.pallas_call(
        finish_kernel,
        out_shape=jax.ShapeDtypeStruct((4, 8, 64, LON), BF16),
        in_specs=[VM],
        out_specs=ANY,
        scratch_shapes=[pltpu.SemaphoreType.DMA((8,))],
        compiler_params=pltpu.CompilerParams(vmem_limit_bytes=1 << 20),
        name="finish",
    )(part)


def local(x, kernel, offset, position, slots, reading, precision):
    part = run_forecast(
        x,
        kernel,
        offset.reshape(1, 64),
        position.reshape(16, 128),
        slots,
        reading.reshape(16, 128),
        precision.reshape(16, 128),
    )
    return run_finish(part)


def solution(mesh):
    return jax.shard_map(
        local,
        mesh=mesh,
        in_specs=(
            P("member", "band", None, None), P(), P(), P("band"), P("band"), P("band"), P("band"),
        ),
        out_specs=P("member", "band", None, None),
        check_vma=False,
    )
```
